32 devices in a mesh: groups: 2 (over y), feat: 4 (over z), layer: 2 (over x), row: 2 (over core).
Axes of the slice: x: 2, y: 2, z: 4, core: 2. Of those that a mesh axis runs over, the one named last changes fastest.
Arguments:
- resid_buf: bfloat16 [512, 2, 4608], P(('groups', 'feat', 'row')), parts along dimension 0, may hold values from -6 to 6
- shuffle: int32 [512], P('groups'), parts along dimension 0, may hold values from 0 to 255, each once
- mlp_out: bfloat16 [512, 2, 4608], P(('groups', 'feat', 'row')), parts along dimension 0, may hold values from -5 to 5
- enc_weight: bfloat16 [2, 8192, 4608], P('layer', 'feat', 'row'), may hold values from -0.09375 to 0.09375
- dec_weight: bfloat16 [2, 8192, 2, 4608], P('layer', 'feat', None, 'row'), may hold values from -0.0625 to 0.0625
- enc_bias: float32 [2, 8192], P('layer', 'feat'), may hold values from -0.5 to 0.5
- dec_bias: float32 [2, 4608], replicated, may hold values from -3 to 3
Outputs:
- rebuilt: bfloat16 [512, 2, 4608], P(('groups', 'feat', 'row')), parts along dimension 0
- enc_grad: bfloat16 [4, 8192, 4608], P(('groups', 'layer'), 'feat', 'row'), parts along dimension 0
- dec_grad: bfloat16 [4, 8192, 2, 4608], P(('groups', 'layer'), 'feat', None, 'row'), parts along dimension 0
- bias_grad: float32 [4, 8192], P(('groups', 'layer'), 'feat'), parts along dimension 0
The draws below stay inside these ranges and needn't reach their ends.
There are 2 independent parts, one for each index of `groups`. The reference program is written for one: setup_inputs(seed, part) draws one part's arguments, and reference() takes and returns one part's arrays. A program takes and returns all parts, laid end to end along the dimension named above; an argument that names none is the same for every part. Nothing has to cross between parts.
Inputs may be any that keep to these rules, and one draw needn't show every extreme that they name: `shuffle`: a permutation of the 256 buffer rows.
All inputs are finite; a program needn't handle non-finite values.
Results may differ from the reference program's by a relative error of at most 0.04.
Values may be sent and summed in bfloat16 or wider, within the bound.
A program may use at most 128 MiB of HBM per device.

```python
import jax
import jax.numpy as jnp

D = 4608
F = 8192
LAYERS = 2
ROWS = 256
FSEC = 8192
N_LAYER = 2


def steps_of(rng, shape, pieces, smallest, largest):
    def one(position, shards_of):
        steps = jax.random.uniform(jax.random.fold_in(jax.random.fold_in(rng, 6), position), (shards_of,), jnp.float32, smallest / len(pieces), largest / len(pieces))
        return jnp.repeat(jnp.exp(steps), shape[position] // shards_of).reshape((-1,) + (1,) * (len(shape) - position - 1))

    gain = one(*pieces[0])
    for cut in pieces[1:]:
        gain = gain * one(*cut)
    return gain


def centred(rng, shape, scale, limit, pieces=(), held_as=jnp.bfloat16):
    array = jax.random.normal(rng, shape, jnp.float32) * scale
    if len(pieces) > 0:
        array = steps_of(rng, shape, pieces, -0.22, 0.18) * array
    return jnp.clip(array, min=-limit, max=limit).astype(held_as)


def setup_inputs(seed: int = 0, part: int = 0) -> dict:
    seeds = jax.random.split(jax.random.key(seed), 8)
    own_keys = jax.random.split(jax.random.fold_in(seeds[7], part), 8)
    resid_buf = centred(own_keys[0], (ROWS, LAYERS, D), 1.0, 6.0, ((0, 8),))
    shuffle = jax.random.permutation(own_keys[1], ROWS).astype(jnp.int32)
    mlp_out = centred(own_keys[2], (ROWS, LAYERS, D), 0.7, 5.0, ((0, 8),))
    enc_weight = centred(seeds[3], (N_LAYER, FSEC, D), D ** -0.5, 0.09375, ((0, 2), (1, 4), (2, 2)))
    dec_weight = centred(seeds[4], (N_LAYER, FSEC, 2, D), F ** -0.5, 0.0625, ((0, 2), (1, 4), (3, 2)))
    enc_bias = jnp.clip(jax.random.uniform(seeds[5], (N_LAYER, FSEC), jnp.float32, -0.5, 0.5) * steps_of(seeds[5], (N_LAYER, FSEC), ((0, 2), (1, 4)), -0.4, 0.0), -0.5, 0.5)
    dec_bias = centred(seeds[6], (LAYERS, D), 0.5, 3.0, (), jnp.float32)
    return {"resid_buf": resid_buf, "shuffle": shuffle, "mlp_out": mlp_out, "enc_weight": enc_weight, "dec_weight": dec_weight, "enc_bias": enc_bias, "dec_bias": dec_bias}


def reference(resid_buf, shuffle, mlp_out, enc_weight, dec_weight, enc_bias, dec_bias):
    encoders = enc_weight.reshape(LAYERS, F, D)
    decoders = dec_weight.reshape(LAYERS, F, 2, D)
    biases = enc_bias.reshape(LAYERS, F)
    inputs = jnp.take(resid_buf, shuffle.astype(jnp.int32), axis=0)
    loss_scale = float(ROWS) ** -0.5
    pre_list = []
    feature_list = []
    for source in range(LAYERS):
        pre_act = jnp.dot(inputs[:, source], encoders[source].T, preferred_element_type=jnp.float32) + biases[source]
        pre_list.append(pre_act)
        feature_list.append(jnp.maximum(pre_act, 0.0).astype(jnp.bfloat16))
    rebuilt_list = []
    for target in range(LAYERS):
        total = jnp.zeros((ROWS, D), jnp.float32) + dec_bias[target]
        for source in range(target + 1):
            total = total + jnp.dot(feature_list[source], decoders[source, :, target - source], preferred_element_type=jnp.float32)
        rebuilt_list.append(total)
    recon_sum = jnp.stack(rebuilt_list, axis=1)
    errors = (recon_sum - mlp_out.astype(jnp.float32)).astype(jnp.bfloat16)
    enc_list = []
    dec_list = []
    bias_list = []
    for source in range(LAYERS):
        own_err = errors[:, source]
        grad_feats = jnp.dot(own_err, decoders[source, :, 0].T, preferred_element_type=jnp.float32)
        own_dec = loss_scale * jnp.dot(feature_list[source].T, own_err, preferred_element_type=jnp.float32)
        if source + 1 < LAYERS:
            next_err = errors[:, source + 1]
            grad_feats = grad_feats + jnp.dot(next_err, decoders[source, :, 1].T, preferred_element_type=jnp.float32)
            next_dec = loss_scale * jnp.dot(feature_list[source].T, next_err, preferred_element_type=jnp.float32)
        else:
            next_dec = jnp.zeros((F, D), jnp.float32)
        grad_feats = grad_feats * loss_scale
        grad_pre = jnp.where(pre_list[source] > 0, grad_feats, 0.0).astype(jnp.bfloat16)
        enc_list.append(jnp.dot(grad_pre.T, inputs[:, source], preferred_element_type=jnp.float32).astype(jnp.bfloat16))
        dec_list.append(jnp.stack([own_dec, next_dec], axis=1).astype(jnp.bfloat16))
        bias_list.append(jnp.sum(grad_pre.astype(jnp.float32), axis=0))
    enc_grad = jnp.stack(enc_list, axis=0).reshape(N_LAYER, FSEC, D)
    dec_grad = jnp.stack(dec_list, axis=0).reshape(N_LAYER, FSEC, 2, D)
    bias_grad = jnp.stack(bias_list, axis=0).reshape(N_LAYER, FSEC)
    return (recon_sum.astype(jnp.bfloat16), enc_grad, dec_grad, bias_grad)
```

```python
import functools

import jax
import jax.numpy as jnp
from jax import lax
from jax.experimental import pallas as pl
from jax.experimental.pallas import tpu as pltpu
from jax.sharding import PartitionSpec as P

LAYERS = 2


def from_behind(block, axis, distance):
    devices = range(lax.axis_size(axis))
    route = [(i - distance, i) for i in devices if i - distance in devices]
    return lax.ppermute(block, axis, route)


def dot_last(left, right):
    return lax.dot_general(
        left, right, (((1,), (1,)), ((), ())), preferred_element_type=jnp.float32
    )


def dot_first(left, right):
    return lax.dot_general(
        left, right, (((0,), (0,)), ((), ())), preferred_element_type=jnp.float32
    )


def on_device(resid_buf, shuffle, mlp_out, enc_weight, dec_weight, enc_bias, dec_bias):
    feat_count = lax.axis_size("feat")
    row_count = lax.axis_size("row")
    sub_blocks = lax.axis_size("layer") // LAYERS
    layer_pos = lax.axis_index("layer")
    row_pos = lax.axis_index("row")
    source = layer_pos // sub_blocks
    rows_each = resid_buf.shape[0]
    width = dec_bias.shape[1]
    half_width = enc_weight.shape[2]
    local_rows = rows_each * feat_count
    total_rows = local_rows * row_count
    loss_scale = float(total_rows) ** (-0.5)
    own_layer = lax.dynamic_index_in_dim(resid_buf, source, axis=1, keepdims=False)
    buffer_all = lax.all_gather(own_layer, ("feat", "row"), axis=0, tiled=True)
    batch_rows = jnp.take(buffer_all, shuffle, axis=0)
    blocks = batch_rows.reshape(feat_count, row_count, rows_each, width)
    inputs_half = lax.dynamic_slice_in_dim(
        jnp.swapaxes(blocks, 0, 1), row_pos * half_width, half_width, axis=3
    )
    inputs_half = inputs_half.reshape(total_rows, half_width)
    own_half_dec = dec_weight[0][:, 0]
    next_half_dec = dec_weight[0][:, 1]
    pre_all = lax.psum(dot_last(inputs_half, enc_weight[0]), "row") + enc_bias[0]
    features_all = jnp.maximum(pre_all, 0.0).astype(jnp.bfloat16)
    own_part = jnp.dot(features_all, own_half_dec, preferred_element_type=jnp.float32)
    next_part = jnp.dot(features_all, next_half_dec, preferred_element_type=jnp.float32)
    carried = from_behind(next_part, "layer", sub_blocks)
    spread = (own_part + carried).reshape(row_count, local_rows, half_width)
    halves = lax.psum_scatter(spread, "feat", scatter_dimension=1, tiled=True)
    joined = lax.all_to_all(halves, "row", split_axis=0, concat_axis=2, tiled=True)
    section_sum = joined.reshape(rows_each, width)
    target_ids = jnp.arange(LAYERS, dtype=jnp.int32)
    target_slots = jnp.where((target_ids == source)[:, None, None], section_sum[None], 0.0)
    totals = lax.psum(target_slots, "layer")
    recon_sum = jnp.swapaxes(totals, 0, 1) + dec_bias[None]
    errors = (recon_sum - mlp_out.astype(jnp.float32)).astype(jnp.bfloat16)
    gathered = lax.all_gather(errors, ("feat", "row"), axis=0, tiled=True)
    error_grid = gathered.reshape(feat_count, row_count, rows_each, LAYERS, width)
    errors_mine = lax.dynamic_index_in_dim(error_grid, row_pos, axis=1, keepdims=False)
    errors_mine = errors_mine.reshape(local_rows, LAYERS, width)
    errors_half = lax.dynamic_slice_in_dim(
        jnp.swapaxes(error_grid, 0, 1), row_pos * half_width, half_width, axis=4
    )
    errors_half = errors_half.reshape(total_rows, LAYERS, half_width)
    live_next = source + 1 < LAYERS
    next_index = jnp.minimum(source + 1, LAYERS - 1)
    half_own = lax.dynamic_index_in_dim(errors_half, source, axis=1, keepdims=False)
    half_next = lax.dynamic_index_in_dim(errors_half, next_index, axis=1, keepdims=False)
    half_next = jnp.where(live_next, half_next, jnp.zeros_like(half_next))
    half_terms = dot_last(half_own, own_half_dec) + dot_last(half_next, next_half_dec)
    grad_feats = lax.psum(half_terms, "row") * loss_scale
    grad_all = jnp.where(pre_all > 0, grad_feats, 0.0).astype(jnp.bfloat16)
    grad_own = loss_scale * dot_first(features_all, half_own)
    grad_next = loss_scale * dot_first(features_all, half_next)
    enc_grad = dot_first(grad_all, inputs_half).astype(jnp.bfloat16)
    dec_grad = jnp.stack([grad_own, grad_next], axis=1).astype(jnp.bfloat16)
    bias_grad = jnp.sum(grad_all.astype(jnp.float32), axis=0)
    return (recon_sum.astype(jnp.bfloat16), enc_grad[None], dec_grad[None], bias_grad[None])

KC = 256
DC = 128
MESH = pl.DeviceIdType.MESH
VMEM_LIMIT = 67043328
BF = jnp.bfloat16


def pick(rows, cols, stride, offset):
    r = lax.broadcasted_iota(jnp.int32, (rows, cols), 0)
    c = lax.broadcasted_iota(jnp.int32, (rows, cols), 1)
    return (c == stride * r + offset).astype(BF)


def mm(left, right):
    return jnp.dot(left, right, preferred_element_type=jnp.float32)


def step_kernel(
    n, J, res, shuf, mlp, enc, dec, bias, dbias,
    feats, xs, errs, gpre, bgrad, rebuilt,
    enc_v, wv, raw, xsend, xg, mlpx, msend, pre_own, pre_send, pre_recv, fall,
    nsend, nrecv, facc, osend, rrecv, e0, e1, rc, rb, g_own, g_send, g_recv, gall,
    sem_l, sem_raw, x_s, x_r, m_s, m_r, p_s, p_r, f_s, f_r, n_s, n_r, r_s, r_r,
    e_s, e_r, t_s, t_r, b_s, b_r, g_s, g_r, q_s, q_r,
):
    z = lax.axis_index("feat")
    x = lax.axis_index("layer")
    c = lax.axis_index("row")
    R, H = xsend.shape[1:]
    F = enc_v.shape[0]
    T = xs.shape[0]
    T2, CR, NC = T // 2, 2 * R, H // J
    nk = F // KC
    scale = float(T) ** (-0.5)
    other_c, other_x = 1 - c, 1 - x

    def far(dz):
        return lax.rem(z + dz, n)

    def back(dz):
        return lax.rem(z + n - dz, n)

    def remote(src, dst, send, recv, **where):
        return pltpu.make_async_remote_copy(
            src_ref=src, dst_ref=dst, send_sem=send, recv_sem=recv,
            device_id=where, device_id_type=MESH)

    enc_copy = pltpu.make_async_copy(enc, enc_v, sem_l)
    enc_copy.start()

    def raw_copy(i, slot):
        return pltpu.make_async_copy(
            dec.at[pl.ds(pl.multiple_of(i * DC, DC), DC)], raw.at[slot], sem_raw.at[slot])

    raw_copy(0, 0).start()

    barrier = pltpu.get_barrier_semaphore()
    for dz in range(n):
        if dz:
            pl.semaphore_signal(barrier, inc=1, device_id={"feat": far(dz), "row": c}, device_id_type=MESH)
        pl.semaphore_signal(barrier, inc=1, device_id={"feat": far(dz), "row": other_c}, device_id_type=MESH)
    for cc in (c, other_c):
        pl.semaphore_signal(barrier, inc=1, device_id={"layer": other_x, "row": cc}, device_id_type=MESH)

    own_x = mm(pick(R, 2 * R, 2, x), res.reshape(2 * R, 2 * H)[...]).astype(BF)
    x_mine = jnp.where(c == 0, own_x[:, :H], own_x[:, H:])
    xsend[0] = x_mine
    xsend[1] = jnp.where(c == 0, own_x[:, H:], own_x[:, :H])
    xg[z, c] = x_mine
    own_m = mm(pick(R, 2 * R, 2, x), mlp.reshape(2 * R, 2 * H)[...]).astype(BF)
    mlpx[c] = jnp.where(c == 0, own_m[:, :H], own_m[:, H:])
    msend[...] = jnp.where(c == 0, own_m[:, H:], own_m[:, :H])

    pl.semaphore_wait(barrier, 2 * n + 1)

    def x_copy(dz, k):
        return remote(xsend.at[k], xg.at[z, c], x_s.at[dz, k], x_r.at[dz, k],
                      feat=far(dz), row=c if k == 0 else other_c)

    x_list = [(dz, k) for dz in range(n) for k in range(2) if dz or k]
    for dz, k in x_list:
        x_copy(dz, k).start()
    m_copy = remote(msend, mlpx.at[c], m_s, m_r, row=other_c)
    m_copy.start()

    s0, s1 = pick(DC, 2 * DC, 2, 0), pick(DC, 2 * DC, 2, 1)
    nd = F // DC

    def split_body(i, carry):
        slot = lax.rem(i, 2)

        @pl.when(i + 1 < nd)
        def _():
            raw_copy(i + 1, 1 - slot).start()

        raw_copy(i, slot).wait()
        blk = raw.at[slot].reshape(2 * DC, H)[...]
        rows = pl.ds(pl.multiple_of(i * DC, DC), DC)
        wv[0, rows, :] = mm(s0, blk).astype(BF)
        wv[1, rows, :] = mm(s1, blk).astype(BF)
        return carry

    lax.fori_loop(0, nd, split_body, 0)

    for dz, k in x_list:
        x_copy(dz, k).wait_recv()
    perm = (lax.broadcasted_iota(jnp.int32, (T, T), 1) == shuf[...]).astype(BF)

    def perm_body(q, carry):
        cols = pl.ds(pl.multiple_of(q * KC, KC), KC)
        xs[:, cols] = mm(perm, xg[:, :, :, cols].reshape(T, KC)).astype(BF)
        return carry

    lax.fori_loop(0, H // KC, perm_body, 0)
    enc_copy.wait()

    def cols_of(k):
        return pl.ds(pl.multiple_of(k * KC, KC), KC)

    def keep_and_send(v, k, own, send):
        top, bot = v[:T2], v[T2:]
        own[k] = jnp.where(c == 0, top, bot)
        send[k] = jnp.where(c == 0, bot, top)

    def p_copy(k):
        return remote(pre_send.at[k], pre_recv.at[k], p_s.at[k], p_r.at[k], row=other_c)

    def f_copy(k):
        return remote(fall.at[c, k], fall.at[c, k], f_s.at[k], f_r.at[k], row=other_c)

    def pre_body(k, carry):
        keep_and_send(dot_last(xs[...], enc_v[cols_of(k), :]), k, pre_own, pre_send)
        p_copy(k).start()
        return carry

    lax.fori_loop(0, nk, pre_body, 0)

    def feat_body(k, carry):
        p_copy(k).wait_recv()
        v = pre_own[k] + pre_recv[k] + bias[:, cols_of(k)]
        fall[c, k] = jnp.maximum(v, 0.0).astype(BF)
        f_copy(k).start()
        return carry

    lax.fori_loop(0, nk, feat_body, 0)

    def join_body(k, carry):
        f_copy(k).wait_recv()
        feats[:, cols_of(k)] = jnp.concatenate([fall[0, k], fall[1, k]], axis=0)
        return carry

    lax.fori_loop(0, nk, join_body, 0)

    def n_copy(j):
        return remote(nsend.at[j], nrecv.at[j], n_s.at[j], n_r.at[j], layer=other_x)

    def r_copy(j, dz):
        return remote(osend.at[j, far(dz)], rrecv.at[j, dz - 1], r_s.at[j, dz], r_r.at[j, dz], feat=far(dz))

    def e_copy(j, dz):
        return remote(e0.at[j, z], e0.at[j, z], e_s.at[j, dz], e_r.at[j, dz], feat=far(dz))

    def t_copy(j, dz):
        return remote(e0.at[j, back(dz)], e1.at[j, back(dz)], t_s.at[j, dz], t_r.at[j, dz], layer=other_x)

    def spots(j, q):
        wide = pl.ds(pl.multiple_of(j * NC + q * KC, KC), KC)
        return wide, pl.ds(pl.multiple_of(q * KC, KC), KC)

    @pl.when(x == 0)
    def _():
        for j in range(J):
            def next_body(q, carry):
                wide, near = spots(j, q)
                nsend[j, :, near] = mm(feats[...], wv[1, :, wide]).astype(BF)
                return carry

            lax.fori_loop(0, NC // KC, next_body, 0)
            n_copy(j).start()

            def own_body(q, carry):
                wide, near = spots(j, q)
                v = mm(feats[...], wv[0, :, wide]).reshape(n, CR, KC)
                facc[:, :, wide] = v
                osend[j, :, :, near] = v.astype(BF)
                return carry

            lax.fori_loop(0, NC // KC, own_body, 0)
            for dz in range(1, n):
                r_copy(j, dz).start()

    @pl.when(x == 1)
    def _():
        for j in range(J):
            def own_body(q, carry):
                wide, near = spots(j, q)
                facc[:, :, wide] = mm(feats[...], wv[0, :, wide]).reshape(n, CR, KC)
                return carry

            lax.fori_loop(0, NC // KC, own_body, 0)
        for j in range(J):
            n_copy(j).wait_recv()

            def add_body(q, carry):
                wide, near = spots(j, q)
                v = facc[:, :, wide] + nrecv[j, :, near].astype(jnp.float32).reshape(n, CR, KC)
                facc[:, :, wide] = v
                osend[j, :, :, near] = v.astype(BF)
                return carry

            lax.fori_loop(0, NC // KC, add_body, 0)
            for dz in range(1, n):
                r_copy(j, dz).start()

    m_copy.wait_recv()

    def reduce_chunk(j):
        for dz in range(1, n):
            r_copy(j, dz).wait_recv()
        wide = pl.ds(j * NC, NC)
        total = facc[z, :, wide]
        for dz in range(1, n):
            total = total + rrecv[j, dz - 1].astype(jnp.float32)
        d = jnp.where(
            x == 0,
            jnp.where(c == 0, dbias[0:1, j * NC:(j + 1) * NC], dbias[0:1, H + j * NC:H + (j + 1) * NC]),
            jnp.where(c == 0, dbias[1:2, j * NC:(j + 1) * NC], dbias[1:2, H + j * NC:H + (j + 1) * NC]))
        total = total + d
        e0[j, z] = (total - mlpx[:, :, wide].reshape(CR, NC).astype(jnp.float32)).astype(BF)
        for dz in range(1, n):
            e_copy(j, dz).start()

        @pl.when(x == 1)
        def _():
            t_copy(j, 0).start()

        rc[:, j] = total.astype(BF).reshape(2, R, NC)

    def pass_chunk(j):
        for dz in range(1, n):
            e_copy(j, dz).wait_recv()

            @pl.when(x == 1)
            def _():
                t_copy(j, dz).start()

    for j in range(J):
        reduce_chunk(j)
        if j:
            pass_chunk(j - 1)
    pass_chunk(J - 1)

    def b_copy(k):
        dx, dc = k // 2, k % 2
        to_x = other_x if dx else x
        to_c = other_c if dc else c
        return remote(rc.at[to_c], rb.at[x, c], b_s.at[k], b_r.at[k], layer=to_x, row=to_c)

    for k in range(1, 4):
        b_copy(k).start()
    rb[x, c] = rc[c]

    for j in range(J):
        errs[0, :, j * NC:(j + 1) * NC] = e0[j].reshape(T, NC)

    @pl.when(x == 0)
    def _():
        for j in range(J):
            for dz in range(n):
                t_copy(j, dz).wait_recv()
            errs[1, :, j * NC:(j + 1) * NC] = e1[j].reshape(T, NC)

    @pl.when(x == 1)
    def _():
        errs[1] = jnp.zeros((T, H), BF)

    def g_copy(k):
        return remote(g_send.at[k], g_recv.at[k], g_s.at[k], g_r.at[k], row=other_c)

    def q_copy(k):
        return remote(gall.at[c, k], gall.at[c, k], q_s.at[k], q_r.at[k], row=other_c)

    @pl.when(x == 0)
    def _():
        def grad_body(k, carry):
            v = dot_last(errs[0], wv[0, cols_of(k), :]) + dot_last(errs[1], wv[1, cols_of(k), :])
            keep_and_send(v, k, g_own, g_send)
            g_copy(k).start()
            return carry

        lax.fori_loop(0, nk, grad_body, 0)

    @pl.when(x == 1)
    def _():
        def grad_body(k, carry):
            keep_and_send(dot_last(errs[0], wv[0, cols_of(k), :]), k, g_own, g_send)
            g_copy(k).start()
            return carry

        lax.fori_loop(0, nk, grad_body, 0)

    def mask_body(k, carry):
        g_copy(k).wait_recv()
        v = (g_own[k] + g_recv[k]) * scale
        gall[c, k] = jnp.where(fall[c, k].astype(jnp.float32) > 0, v, 0.0).astype(BF)
        q_copy(k).start()
        return carry

    lax.fori_loop(0, nk, mask_body, 0)

    for k in range(1, 4):
        b_copy(k).wait_recv()
    i0, i1 = pick(R, 2 * R, 2, 0).T, pick(R, 2 * R, 2, 1).T
    out = rebuilt.reshape(2 * R, 2 * H)
    for h in range(2):
        for j in range(J):
            lo = h * H + j * NC
            out[:, lo:lo + NC] = (mm(i0, rb[0, h, j]) + mm(i1, rb[1, h, j])).astype(BF)

    def last_body(k, carry):
        q_copy(k).wait_recv()
        both = jnp.concatenate([gall[0, k], gall[1, k]], axis=0)
        gpre[:, cols_of(k)] = both
        bgrad[:, cols_of(k)] = jnp.sum(both.astype(jnp.float32), axis=0, keepdims=True)
        p_copy(k).wait_send()
        f_copy(k).wait_send()
        g_copy(k).wait_send()
        q_copy(k).wait_send()
        return carry

    lax.fori_loop(0, nk, last_body, 0)

    for dz, k in x_list:
        x_copy(dz, k).wait_send()
    m_copy.wait_send()
    for j in range(J):
        for dz in range(1, n):
            r_copy(j, dz).wait_send()
            e_copy(j, dz).wait_send()
    for k in range(1, 4):
        b_copy(k).wait_send()

    @pl.when(x == 0)
    def _():
        for j in range(J):
            n_copy(j).wait_send()

    @pl.when(x == 1)
    def _():
        for j in range(J):
            for dz in range(n):
                t_copy(j, dz).wait_send()


def weight_kernel(scale, feats, gpre, errs, xs, enc_grad, dec_grad):
    fc, H = enc_grad.shape
    f = feats[...]
    enc_grad[...] = dot_first(gpre[...], xs[...]).astype(BF)
    g = dot_first(mm(f, pick(fc, 2 * fc, 2, 0)).astype(BF), errs[0])
    g = g + dot_first(mm(f, pick(fc, 2 * fc, 2, 1)).astype(BF), errs[1])
    dec_grad.reshape(2 * fc, H)[...] = (scale * g).astype(BF)


def fused(resid_buf, shuffle, mlp_out, enc_weight, dec_weight, enc_bias, dec_bias):
    n = lax.axis_size("feat")
    R = resid_buf.shape[0]
    F, H = enc_weight.shape[1:]
    T = R * n * 2
    T2, CR = T // 2, 2 * R
    J = 3 if H % (3 * KC) == 0 else 1
    NC, nk = H // J, F // KC
    f32 = jnp.float32
    vm = pl.BlockSpec(memory_space=pltpu.VMEM)
    hbm = pl.BlockSpec(memory_space=pl.ANY)
    dma = pltpu.SemaphoreType.DMA
    shape = jax.ShapeDtypeStruct
    feats, xs, errs, gpre, bgrad, rebuilt = pl.pallas_call(
        functools.partial(step_kernel, n, J),
        out_shape=(
            shape((T, F), BF), shape((T, H), BF), shape((2, T, H), BF), shape((T, F), BF),
            shape((1, F), f32), shape((R, 2, 2 * H), BF)),
        in_specs=[vm, vm, vm, hbm, hbm, vm, vm],
        out_specs=[vm] * 6,
        scratch_shapes=[
            pltpu.VMEM((F, H), BF), pltpu.VMEM((2, F, H), BF), pltpu.VMEM((2, DC, 2, H), BF),
            pltpu.VMEM((2, R, H), BF), pltpu.VMEM((n, 2, R, H), BF),
            pltpu.VMEM((2, R, H), BF), pltpu.VMEM((R, H), BF),
            pltpu.VMEM((nk, T2, KC), f32), pltpu.VMEM((nk, T2, KC), f32), pltpu.VMEM((nk, T2, KC), f32),
            pltpu.VMEM((2, nk, T2, KC), BF),
            pltpu.VMEM((J, T, NC), BF), pltpu.VMEM((J, T, NC), BF), pltpu.VMEM((n, CR, H), f32),
            pltpu.VMEM((J, n, CR, NC), BF), pltpu.VMEM((J, n - 1, CR, NC), BF),
            pltpu.VMEM((J, n, CR, NC), BF), pltpu.VMEM((J, n, CR, NC), BF),
            pltpu.VMEM((2, J, R, NC), BF), pltpu.VMEM((2, 2, J, R, NC), BF),
            pltpu.VMEM((nk, T2, KC), f32), pltpu.VMEM((nk, T2, KC), f32), pltpu.VMEM((nk, T2, KC), f32),
            pltpu.VMEM((2, nk, T2, KC), BF),
            dma, dma((2,)), dma((n, 2)), dma((n, 2)), dma, dma, dma((nk,)), dma((nk,)),
            dma((nk,)), dma((nk,)), dma((J,)), dma((J,)), dma((J, n)), dma((J, n)),
            dma((J, n)), dma((J, n)), dma((J, n)), dma((J, n)), dma((4,)), dma((4,)),
            dma((nk,)), dma((nk,)), dma((nk,)), dma((nk,)),
        ],
        compiler_params=pltpu.CompilerParams(
            collective_id=0, has_side_effects=True, vmem_limit_bytes=VMEM_LIMIT),
    )(resid_buf, shuffle.reshape(T, 1), mlp_out, enc_weight[0], dec_weight[0], enc_bias, dec_bias)
    fc = 128
    enc_grad, dec_grad = pl.pallas_call(
        functools.partial(weight_kernel, float(T) ** (-0.5)),
        grid=(F // fc,),
        out_shape=(shape((F, H), BF), shape((F, 2, H), BF)),
        in_specs=[
            pl.BlockSpec((T, fc), lambda i: (0, i)), pl.BlockSpec((T, fc), lambda i: (0, i)),
            pl.BlockSpec((2, T, H), lambda i: (0, 0, 0)), pl.BlockSpec((T, H), lambda i: (0, 0))],
        out_specs=(
            pl.BlockSpec((fc, H), lambda i: (i, 0)), pl.BlockSpec((fc, 2, H), lambda i: (i, 0, 0))),
        compiler_params=pltpu.CompilerParams(vmem_limit_bytes=VMEM_LIMIT),
    )(feats, gpre, errs, xs)
    return rebuilt, enc_grad[None], dec_grad[None], bgrad


def chosen(resid_buf, shuffle, mlp_out, enc_weight, dec_weight, enc_bias, dec_bias):
    args = (resid_buf, shuffle, mlp_out, enc_weight, dec_weight, enc_bias, dec_bias)
    rows, width = resid_buf.shape[0], enc_weight.shape[2]
    fits = (
        lax.axis_size("layer") == LAYERS == 2 and lax.axis_size("row") == 2
        and 1 < lax.axis_size("feat") <= 4 and rows % 16 == 0
        and width % KC == 0 and enc_weight.shape[1] % KC == 0)
    return fused(*args) if fits else on_device(*args)


def solution(mesh):
    return jax.shard_map(
        chosen,
        mesh=mesh,
        in_specs=(
            P(("groups", "feat", "row"), None, None),
            P("groups"),
            P(("groups", "feat", "row"), None, None),
            P("layer", "feat", "row"),
            P("layer", "feat", None, "row"),
            P("layer", "feat"),
            P(),
        ),
        out_specs=(
            P(("groups", "feat", "row"), None, None),
            P(("groups", "layer"), "feat", "row"),
            P(("groups", "layer"), "feat", None, "row"),
            P(("groups", "layer"), "feat"),
        ),
        check_vma=False,
    )
```

```python
import functools

import jax
import jax.numpy as jnp
from jax import lax
from jax.experimental import pallas as pl
from jax.experimental.pallas import tpu as pltpu
from jax.sharding import PartitionSpec as P

LAYERS = 2


def from_behind(block, axis, distance):
    devices = range(lax.axis_size(axis))
    route = [(i - distance, i) for i in devices if i - distance in devices]
    return lax.ppermute(block, axis, route)


def dot_last(left, right):
    return lax.dot_general(
        left, right, (((1,), (1,)), ((), ())), preferred_element_type=jnp.float32
    )


def dot_first(left, right):
    return lax.dot_general(
        left, right, (((0,), (0,)), ((), ())), preferred_element_type=jnp.float32
    )


def on_device(resid_buf, shuffle, mlp_out, enc_weight, dec_weight, enc_bias, dec_bias):
    feat_count = lax.axis_size("feat")
    row_count = lax.axis_size("row")
    sub_blocks = lax.axis_size("layer") // LAYERS
    layer_pos = lax.axis_index("layer")
    row_pos = lax.axis_index("row")
    source = layer_pos // sub_blocks
    rows_each = resid_buf.shape[0]
    width = dec_bias.shape[1]
    half_width = enc_weight.shape[2]
    local_rows = rows_each * feat_count
    total_rows = local_rows * row_count
    loss_scale = float(total_rows) ** (-0.5)
    own_layer = lax.dynamic_index_in_dim(resid_buf, source, axis=1, keepdims=False)
    buffer_all = lax.all_gather(own_layer, ("feat", "row"), axis=0, tiled=True)
    batch_rows = jnp.take(buffer_all, shuffle, axis=0)
    blocks = batch_rows.reshape(feat_count, row_count, rows_each, width)
    inputs_half = lax.dynamic_slice_in_dim(
        jnp.swapaxes(blocks, 0, 1), row_pos * half_width, half_width, axis=3
    )
    inputs_half = inputs_half.reshape(total_rows, half_width)
    own_half_dec = dec_weight[0][:, 0]
    next_half_dec = dec_weight[0][:, 1]
    pre_all = lax.psum(dot_last(inputs_half, enc_weight[0]), "row") + enc_bias[0]
    features_all = jnp.maximum(pre_all, 0.0).astype(jnp.bfloat16)
    own_part = jnp.dot(features_all, own_half_dec, preferred_element_type=jnp.float32)
    next_part = jnp.dot(features_all, next_half_dec, preferred_element_type=jnp.float32)
    carried = from_behind(next_part, "layer", sub_blocks)
    spread = (own_part + carried).reshape(row_count, local_rows, half_width)
    halves = lax.psum_scatter(spread, "feat", scatter_dimension=1, tiled=True)
    joined = lax.all_to_all(halves, "row", split_axis=0, concat_axis=2, tiled=True)
    section_sum = joined.reshape(rows_each, width)
    target_ids = jnp.arange(LAYERS, dtype=jnp.int32)
    target_slots = jnp.where((target_ids == source)[:, None, None], section_sum[None], 0.0)
    totals = lax.psum(target_slots, "layer")
    recon_sum = jnp.swapaxes(totals, 0, 1) + dec_bias[None]
    errors = (recon_sum - mlp_out.astype(jnp.float32)).astype(jnp.bfloat16)
    gathered = lax.all_gather(errors, ("feat", "row"), axis=0, tiled=True)
    error_grid = gathered.reshape(feat_count, row_count, rows_each, LAYERS, width)
    errors_mine = lax.dynamic_index_in_dim(error_grid, row_pos, axis=1, keepdims=False)
    errors_mine = errors_mine.reshape(local_rows, LAYERS, width)
    errors_half = lax.dynamic_slice_in_dim(
        jnp.swapaxes(error_grid, 0, 1), row_pos * half_width, half_width, axis=4
    )
    errors_half = errors_half.reshape(total_rows, LAYERS, half_width)
    live_next = source + 1 < LAYERS
    next_index = jnp.minimum(source + 1, LAYERS - 1)
    half_own = lax.dynamic_index_in_dim(errors_half, source, axis=1, keepdims=False)
    half_next = lax.dynamic_index_in_dim(errors_half, next_index, axis=1, keepdims=False)
    half_next = jnp.where(live_next, half_next, jnp.zeros_like(half_next))
    half_terms = dot_last(half_own, own_half_dec) + dot_last(half_next, next_half_dec)
    grad_feats = lax.psum(half_terms, "row") * loss_scale
    grad_all = jnp.where(pre_all > 0, grad_feats, 0.0).astype(jnp.bfloat16)
    grad_own = loss_scale * dot_first(features_all, half_own)
    grad_next = loss_scale * dot_first(features_all, half_next)
    enc_grad = dot_first(grad_all, inputs_half).astype(jnp.bfloat16)
    dec_grad = jnp.stack([grad_own, grad_next], axis=1).astype(jnp.bfloat16)
    bias_grad = jnp.sum(grad_all.astype(jnp.float32), axis=0)
    return (recon_sum.astype(jnp.bfloat16), enc_grad[None], dec_grad[None], bias_grad[None])

KC = 256
DC = 128
MESH = pl.DeviceIdType.MESH
VMEM_LIMIT = 67043328
BF = jnp.bfloat16


def pick(rows, cols, stride, offset):
    r = lax.broadcasted_iota(jnp.int32, (rows, cols), 0)
    c = lax.broadcasted_iota(jnp.int32, (rows, cols), 1)
    return (c == stride * r + offset).astype(BF)


def mm(left, right):
    return jnp.dot(left, right, preferred_element_type=jnp.float32)


def step_kernel(
    n, J, res, shuf, mlp, enc, dec, bias, dbias,
    feats, xs, errs, gpre, parts,
    enc_v, wv, raw, xsend, xg, mlpx, msend, pre_own, pre_send, pre_recv, fall,
    nsend, nrecv, facc, osend, rrecv, e0, e1, rc, rb, g_own, g_send, g_recv, gall,
    sem_l, sem_raw, x_s, x_r, m_s, m_r, p_s, p_r, f_s, f_r, n_s, n_r, r_s, r_r,
    e_s, e_r, t_s, t_r, b_s, b_r, g_s, g_r, q_s, q_r,
):
    z = lax.axis_index("feat")
    x = lax.axis_index("layer")
    c = lax.axis_index("row")
    R, H = xsend.shape[1:]
    F = enc_v.shape[0]
    T = xs.shape[0]
    T2, CR, NC = T // 2, 2 * R, H // J
    nk = F // KC
    scale = float(T) ** (-0.5)
    other_c, other_x = 1 - c, 1 - x

    def far(dz):
        return lax.rem(z + dz, n)

    def back(dz):
        return lax.rem(z + n - dz, n)

    def remote(src, dst, send, recv, **where):
        return pltpu.make_async_remote_copy(
            src_ref=src, dst_ref=dst, send_sem=send, recv_sem=recv,
            device_id=where, device_id_type=MESH)

    enc_copy = pltpu.make_async_copy(enc, enc_v, sem_l)
    enc_copy.start()

    def raw_copy(i, slot):
        return pltpu.make_async_copy(
            dec.at[pl.ds(pl.multiple_of(i * DC, DC), DC)], raw.at[slot], sem_raw.at[slot])

    raw_copy(0, 0).start()

    barrier = pltpu.get_barrier_semaphore()
    for dz in range(n):
        if dz:
            pl.semaphore_signal(barrier, inc=1, device_id={"feat": far(dz), "row": c}, device_id_type=MESH)
        pl.semaphore_signal(barrier, inc=1, device_id={"feat": far(dz), "row": other_c}, device_id_type=MESH)
    for cc in (c, other_c):
        pl.semaphore_signal(barrier, inc=1, device_id={"layer": other_x, "row": cc}, device_id_type=MESH)

    own_x = mm(pick(R, 2 * R, 2, x), res.reshape(2 * R, 2 * H)[...]).astype(BF)
    x_mine = jnp.where(c == 0, own_x[:, :H], own_x[:, H:])
    xsend[0] = x_mine
    xsend[1] = jnp.where(c == 0, own_x[:, H:], own_x[:, :H])
    xg[z, c] = x_mine
    own_m = mm(pick(R, 2 * R, 2, x), mlp.reshape(2 * R, 2 * H)[...]).astype(BF)
    mlpx[c] = jnp.where(c == 0, own_m[:, :H], own_m[:, H:])
    msend[...] = jnp.where(c == 0, own_m[:, H:], own_m[:, :H])

    pl.semaphore_wait(barrier, 2 * n + 1)

    def x_copy(dz, k):
        return remote(xsend.at[k], xg.at[z, c], x_s.at[dz, k], x_r.at[dz, k],
                      feat=far(dz), row=c if k == 0 else other_c)

    x_list = [(dz, k) for dz in range(n) for k in range(2) if dz or k]
    for dz, k in x_list:
        x_copy(dz, k).start()
    m_copy = remote(msend, mlpx.at[c], m_s, m_r, row=other_c)
    m_copy.start()

    s0, s1 = pick(DC, 2 * DC, 2, 0), pick(DC, 2 * DC, 2, 1)
    nd = F // DC

    def split_body(i, carry):
        slot = lax.rem(i, 2)

        @pl.when(i + 1 < nd)
        def _():
            raw_copy(i + 1, 1 - slot).start()

        raw_copy(i, slot).wait()
        blk = raw.at[slot].reshape(2 * DC, H)[...]
        rows = pl.ds(pl.multiple_of(i * DC, DC), DC)
        wv[0, rows, :] = mm(s0, blk).astype(BF)
        wv[1, rows, :] = mm(s1, blk).astype(BF)
        return carry

    lax.fori_loop(0, nd, split_body, 0)

    for dz, k in x_list:
        x_copy(dz, k).wait_recv()
    perm = (lax.broadcasted_iota(jnp.int32, (T, T), 0) == shuf[...]).astype(BF)

    def perm_body(q, carry):
        cols = pl.ds(pl.multiple_of(q * KC, KC), KC)
        xs[:, cols] = dot_first(perm, xg[:, :, :, cols].reshape(T, KC)).astype(BF)
        return carry

    lax.fori_loop(0, H // KC, perm_body, 0)
    enc_copy.wait()

    def cols_of(k):
        return pl.ds(pl.multiple_of(k * KC, KC), KC)

    def keep_and_send(v, k, own, send):
        top, bot = v[:T2], v[T2:]
        own[k] = jnp.where(c == 0, top, bot)
        send[k] = jnp.where(c == 0, bot, top)

    def p_copy(k):
        return remote(pre_send.at[k], pre_recv.at[k], p_s.at[k], p_r.at[k], row=other_c)

    def f_copy(k):
        return remote(fall.at[c, k], fall.at[c, k], f_s.at[k], f_r.at[k], row=other_c)

    def pre_body(k, carry):
        keep_and_send(dot_last(xs[...], enc_v[cols_of(k), :]), k, pre_own, pre_send)
        p_copy(k).start()
        return carry

    lax.fori_loop(0, nk, pre_body, 0)

    def feat_body(k, carry):
        p_copy(k).wait_recv()
        v = pre_own[k] + pre_recv[k] + bias[:, cols_of(k)]
        fall[c, k] = jnp.maximum(v, 0.0).astype(BF)
        f_copy(k).start()
        return carry

    lax.fori_loop(0, nk, feat_body, 0)

    def join_body(k, carry):
        f_copy(k).wait_recv()
        feats[:, cols_of(k)] = jnp.concatenate([fall[0, k], fall[1, k]], axis=0)
        return carry

    lax.fori_loop(0, nk, join_body, 0)

    def n_copy(j):
        return remote(nsend.at[j], nrecv.at[j], n_s.at[j], n_r.at[j], layer=other_x)

    def r_copy(j, dz):
        return remote(osend.at[j, far(dz)], rrecv.at[j, dz - 1], r_s.at[j, dz], r_r.at[j, dz], feat=far(dz))

    def e_copy(j, dz):
        return remote(e0.at[j, z], e0.at[j, z], e_s.at[j, dz], e_r.at[j, dz], feat=far(dz))

    def t_copy(j, dz):
        return remote(e0.at[j, back(dz)], e1.at[j, back(dz)], t_s.at[j, dz], t_r.at[j, dz], layer=other_x)

    def spots(j, q):
        wide = pl.ds(pl.multiple_of(j * NC + q * KC, KC), KC)
        return wide, pl.ds(pl.multiple_of(q * KC, KC), KC)

    @pl.when(x == 0)
    def _():
        for j in range(J):
            def next_body(q, carry):
                wide, near = spots(j, q)
                nsend[j, :, near] = mm(feats[...], wv[1, :, wide]).astype(BF)
                return carry

            lax.fori_loop(0, NC // KC, next_body, 0)
            n_copy(j).start()

            def own_body(q, carry):
                wide, near = spots(j, q)
                v = mm(feats[...], wv[0, :, wide]).reshape(n, CR, KC)
                facc[:, :, wide] = v
                osend[j, :, :, near] = v.astype(BF)
                return carry

            lax.fori_loop(0, NC // KC, own_body, 0)
            for dz in range(1, n):
                r_copy(j, dz).start()

    @pl.when(x == 1)
    def _():
        for j in range(J):
            def own_body(q, carry):
                wide, near = spots(j, q)
                facc[:, :, wide] = mm(feats[...], wv[0, :, wide]).reshape(n, CR, KC)
                return carry

            lax.fori_loop(0, NC // KC, own_body, 0)
        for j in range(J):
            n_copy(j).wait_recv()

            def add_body(q, carry):
                wide, near = spots(j, q)
                v = facc[:, :, wide] + nrecv[j, :, near].astype(jnp.float32).reshape(n, CR, KC)
                facc[:, :, wide] = v
                osend[j, :, :, near] = v.astype(BF)
                return carry

            lax.fori_loop(0, NC // KC, add_body, 0)
            for dz in range(1, n):
                r_copy(j, dz).start()

    m_copy.wait_recv()

    def reduce_chunk(j):
        for dz in range(1, n):
            r_copy(j, dz).wait_recv()
        wide = pl.ds(j * NC, NC)
        total = facc[z, :, wide]
        for dz in range(1, n):
            total = total + rrecv[j, dz - 1].astype(jnp.float32)
        d = jnp.where(
            x == 0,
            jnp.where(c == 0, dbias[0:1, j * NC:(j + 1) * NC], dbias[0:1, H + j * NC:H + (j + 1) * NC]),
            jnp.where(c == 0, dbias[1:2, j * NC:(j + 1) * NC], dbias[1:2, H + j * NC:H + (j + 1) * NC]))
        total = total + d
        e0[j, z] = (total - mlpx[:, :, wide].reshape(CR, NC).astype(jnp.float32)).astype(BF)
        for dz in range(1, n):
            e_copy(j, dz).start()

        @pl.when(x == 1)
        def _():
            t_copy(j, 0).start()

        rc[:, j] = total.astype(BF).reshape(2, R, NC)

    def pass_chunk(j):
        for dz in range(1, n):
            e_copy(j, dz).wait_recv()

            @pl.when(x == 1)
            def _():
                t_copy(j, dz).start()

    for j in range(J):
        reduce_chunk(j)
        if j:
            pass_chunk(j - 1)
    pass_chunk(J - 1)

    def b_copy(k):
        dx, dc = k // 2, k % 2
        to_x = other_x if dx else x
        to_c = other_c if dc else c
        return remote(rc.at[to_c], rb.at[x, c], b_s.at[k], b_r.at[k], layer=to_x, row=to_c)

    for k in range(1, 4):
        b_copy(k).start()
    rb[x, c] = rc[c]

    for j in range(J):
        errs[0, :, j * NC:(j + 1) * NC] = e0[j].reshape(T, NC)

    @pl.when(x == 0)
    def _():
        for j in range(J):
            for dz in range(n):
                t_copy(j, dz).wait_recv()
            errs[1, :, j * NC:(j + 1) * NC] = e1[j].reshape(T, NC)

    @pl.when(x == 1)
    def _():
        errs[1] = jnp.zeros((T, H), BF)

    def g_copy(k):
        return remote(g_send.at[k], g_recv.at[k], g_s.at[k], g_r.at[k], row=other_c)

    def q_copy(k):
        return remote(gall.at[c, k], gall.at[c, k], q_s.at[k], q_r.at[k], row=other_c)

    @pl.when(x == 0)
    def _():
        def grad_body(k, carry):
            v = dot_last(errs[0], wv[0, cols_of(k), :]) + dot_last(errs[1], wv[1, cols_of(k), :])
            keep_and_send(v, k, g_own, g_send)
            g_copy(k).start()
            return carry

        lax.fori_loop(0, nk, grad_body, 0)

    @pl.when(x == 1)
    def _():
        def grad_body(k, carry):
            keep_and_send(dot_last(errs[0], wv[0, cols_of(k), :]), k, g_own, g_send)
            g_copy(k).start()
            return carry

        lax.fori_loop(0, nk, grad_body, 0)

    def mask_body(k, carry):
        g_copy(k).wait_recv()
        v = (g_own[k] + g_recv[k]) * scale
        gall[c, k] = jnp.where(fall[c, k].astype(jnp.float32) > 0, v, 0.0).astype(BF)
        q_copy(k).start()
        return carry

    lax.fori_loop(0, nk, mask_body, 0)

    for k in range(1, 4):
        b_copy(k).wait_recv()
    for h in range(2):
        for j in range(J):
            lo = h * H + j * NC
            parts[:, lo:lo + NC] = rb[:, h, j].reshape(2 * R, NC)

    def last_body(k, carry):
        q_copy(k).wait_recv()
        both = jnp.concatenate([gall[0, k], gall[1, k]], axis=0)
        gpre[:, cols_of(k)] = both
        p_copy(k).wait_send()
        f_copy(k).wait_send()
        g_copy(k).wait_send()
        q_copy(k).wait_send()
        return carry

    lax.fori_loop(0, nk, last_body, 0)

    for dz, k in x_list:
        x_copy(dz, k).wait_send()
    m_copy.wait_send()
    for j in range(J):
        for dz in range(1, n):
            r_copy(j, dz).wait_send()
            e_copy(j, dz).wait_send()
    for k in range(1, 4):
        b_copy(k).wait_send()

    @pl.when(x == 0)
    def _():
        for j in range(J):
            n_copy(j).wait_send()

    @pl.when(x == 1)
    def _():
        for j in range(J):
            for dz in range(n):
                t_copy(j, dz).wait_send()


def weight_kernel(scale, feats, gpre, errs, xs, parts, enc_grad, dec_grad, bgrad, rebuilt):
    fc, H = enc_grad.shape
    R2 = parts.shape[0]

    @pl.when(pl.program_id(0) == 0)
    def _():
        i = lax.broadcasted_iota(jnp.int32, (R2, R2), 0)
        j = lax.broadcasted_iota(jnp.int32, (R2, R2), 1)
        inter = (j == (i % 2) * (R2 // 2) + i // 2).astype(BF)
        rebuilt.reshape(R2, 2 * H)[...] = mm(inter, parts[...]).astype(BF)

    bgrad[...] = jnp.sum(gpre[...].astype(jnp.float32), axis=0, keepdims=True)
    enc_grad[...] = dot_first(gpre[...], xs[...]).astype(BF)
    p0, p1 = pick(DC, 2 * DC, 2, 0), pick(DC, 2 * DC, 2, 1)
    out = dec_grad.reshape(2 * fc, H)
    for b in range(fc // DC):
        f = feats[:, b * DC:(b + 1) * DC]
        g = dot_first(mm(f, p0).astype(BF), errs[0]) + dot_first(mm(f, p1).astype(BF), errs[1])
        out[b * 2 * DC:(b + 1) * 2 * DC, :] = (scale * g).astype(BF)


def fused(resid_buf, shuffle, mlp_out, enc_weight, dec_weight, enc_bias, dec_bias):
    n = lax.axis_size("feat")
    R = resid_buf.shape[0]
    F, H = enc_weight.shape[1:]
    T = R * n * 2
    T2, CR = T // 2, 2 * R
    J = H // KC
    NC, nk = H // J, F // KC
    f32 = jnp.float32
    vm = pl.BlockSpec(memory_space=pltpu.VMEM)
    hbm = pl.BlockSpec(memory_space=pl.ANY)
    dma = pltpu.SemaphoreType.DMA
    shape = jax.ShapeDtypeStruct
    feats, xs, errs, gpre, parts = pl.pallas_call(
        functools.partial(step_kernel, n, J),
        out_shape=(
            shape((T, F), BF), shape((T, H), BF), shape((2, T, H), BF), shape((T, F), BF),
            shape((2 * R, 2 * H), BF)),
        in_specs=[vm, vm, vm, hbm, hbm, vm, vm],
        out_specs=[vm] * 5,
        scratch_shapes=[
            pltpu.VMEM((F, H), BF), pltpu.VMEM((2, F, H), BF), pltpu.VMEM((2, DC, 2, H), BF),
            pltpu.VMEM((2, R, H), BF), pltpu.VMEM((n, 2, R, H), BF),
            pltpu.VMEM((2, R, H), BF), pltpu.VMEM((R, H), BF),
            pltpu.VMEM((nk, T2, KC), f32), pltpu.VMEM((nk, T2, KC), f32), pltpu.VMEM((nk, T2, KC), f32),
            pltpu.VMEM((2, nk, T2, KC), BF),
            pltpu.VMEM((J, T, NC), BF), pltpu.VMEM((J, T, NC), BF), pltpu.VMEM((n, CR, H), f32),
            pltpu.VMEM((J, n, CR, NC), BF), pltpu.VMEM((J, n - 1, CR, NC), BF),
            pltpu.VMEM((J, n, CR, NC), BF), pltpu.VMEM((J, n, CR, NC), BF),
            pltpu.VMEM((2, J, R, NC), BF), pltpu.VMEM((2, 2, J, R, NC), BF),
            pltpu.VMEM((nk, T2, KC), f32), pltpu.VMEM((nk, T2, KC), f32), pltpu.VMEM((nk, T2, KC), f32),
            pltpu.VMEM((2, nk, T2, KC), BF),
            dma, dma((2,)), dma((n, 2)), dma((n, 2)), dma, dma, dma((nk,)), dma((nk,)),
            dma((nk,)), dma((nk,)), dma((J,)), dma((J,)), dma((J, n)), dma((J, n)),
            dma((J, n)), dma((J, n)), dma((J, n)), dma((J, n)), dma((4,)), dma((4,)),
            dma((nk,)), dma((nk,)), dma((nk,)), dma((nk,)),
        ],
        compiler_params=pltpu.CompilerParams(
            collective_id=0, has_side_effects=True, vmem_limit_bytes=VMEM_LIMIT),
    )(resid_buf, shuffle.reshape(1, T), mlp_out, enc_weight[0], dec_weight[0], enc_bias, dec_bias)
    fc = 512 if F % 512 == 0 else KC
    enc_grad, dec_grad, bgrad, rebuilt = pl.pallas_call(
        functools.partial(weight_kernel, float(T) ** (-0.5)),
        grid=(F // fc,),
        out_shape=(
            shape((F, H), BF), shape((F, 2, H), BF), shape((1, F), f32), shape((R, 2, 2 * H), BF)),
        in_specs=[
            pl.BlockSpec((T, fc), lambda i: (0, i)), pl.BlockSpec((T, fc), lambda i: (0, i)),
            pl.BlockSpec((2, T, H), lambda i: (0, 0, 0)), pl.BlockSpec((T, H), lambda i: (0, 0)),
            pl.BlockSpec((2 * R, 2 * H), lambda i: (0, 0))],
        out_specs=(
            pl.BlockSpec((fc, H), lambda i: (i, 0)), pl.BlockSpec((fc, 2, H), lambda i: (i, 0, 0)),
            pl.BlockSpec((1, fc), lambda i: (0, i)), pl.BlockSpec((R, 2, 2 * H), lambda i: (0, 0, 0))),
        compiler_params=pltpu.CompilerParams(vmem_limit_bytes=VMEM_LIMIT),
    )(feats, gpre, errs, xs, parts)
    return rebuilt, enc_grad[None], dec_grad[None], bgrad


def chosen(resid_buf, shuffle, mlp_out, enc_weight, dec_weight, enc_bias, dec_bias):
    args = (resid_buf, shuffle, mlp_out, enc_weight, dec_weight, enc_bias, dec_bias)
    rows, width = resid_buf.shape[0], enc_weight.shape[2]
    fits = (
        lax.axis_size("layer") == LAYERS == 2 and lax.axis_size("row") == 2
        and 1 < lax.axis_size("feat") <= 4 and rows % 16 == 0
        and width % KC == 0 and enc_weight.shape[1] % KC == 0)
    return fused(*args) if fits else on_device(*args)


def solution(mesh):
    return jax.shard_map(
        chosen,
        mesh=mesh,
        in_specs=(
            P(("groups", "feat", "row"), None, None),
            P("groups"),
            P(("groups", "feat", "row"), None, None),
            P("layer", "feat", "row"),
            P("layer", "feat", None, "row"),
            P("layer", "feat"),
            P(),
        ),
        out_specs=(
            P(("groups", "feat", "row"), None, None),
            P(("groups", "layer"), "feat", "row"),
            P(("groups", "layer"), "feat", None, "row"),
            P(("groups", "layer"), "feat"),
        ),
        check_vma=False,
    )
```

```python
import functools

import jax
import jax.numpy as jnp
from jax import lax
from jax.experimental import pallas as pl
from jax.experimental.pallas import tpu as pltpu
from jax.sharding import PartitionSpec as P

LAYERS = 2


def from_behind(block, axis, distance):
    devices = range(lax.axis_size(axis))
    route = [(i - distance, i) for i in devices if i - distance in devices]
    return lax.ppermute(block, axis, route)


def dot_last(left, right):
    return lax.dot_general(
        left, right, (((1,), (1,)), ((), ())), preferred_element_type=jnp.float32
    )


def dot_first(left, right):
    return lax.dot_general(
        left, right, (((0,), (0,)), ((), ())), preferred_element_type=jnp.float32
    )


def on_device(resid_buf, shuffle, mlp_out, enc_weight, dec_weight, enc_bias, dec_bias):
    feat_count = lax.axis_size("feat")
    row_count = lax.axis_size("row")
    sub_blocks = lax.axis_size("layer") // LAYERS
    layer_pos = lax.axis_index("layer")
    row_pos = lax.axis_index("row")
    source = layer_pos // sub_blocks
    rows_each = resid_buf.shape[0]
    width = dec_bias.shape[1]
    half_width = enc_weight.shape[2]
    local_rows = rows_each * feat_count
    total_rows = local_rows * row_count
    loss_scale = float(total_rows) ** (-0.5)
    own_layer = lax.dynamic_index_in_dim(resid_buf, source, axis=1, keepdims=False)
    buffer_all = lax.all_gather(own_layer, ("feat", "row"), axis=0, tiled=True)
    batch_rows = jnp.take(buffer_all, shuffle, axis=0)
    blocks = batch_rows.reshape(feat_count, row_count, rows_each, width)
    inputs_half = lax.dynamic_slice_in_dim(
        jnp.swapaxes(blocks, 0, 1), row_pos * half_width, half_width, axis=3
    )
    inputs_half = inputs_half.reshape(total_rows, half_width)
    own_half_dec = dec_weight[0][:, 0]
    next_half_dec = dec_weight[0][:, 1]
    pre_all = lax.psum(dot_last(inputs_half, enc_weight[0]), "row") + enc_bias[0]
    features_all = jnp.maximum(pre_all, 0.0).astype(jnp.bfloat16)
    own_part = jnp.dot(features_all, own_half_dec, preferred_element_type=jnp.float32)
    next_part = jnp.dot(features_all, next_half_dec, preferred_element_type=jnp.float32)
    carried = from_behind(next_part, "layer", sub_blocks)
    spread = (own_part + carried).reshape(row_count, local_rows, half_width)
    halves = lax.psum_scatter(spread, "feat", scatter_dimension=1, tiled=True)
    joined = lax.all_to_all(halves, "row", split_axis=0, concat_axis=2, tiled=True)
    section_sum = joined.reshape(rows_each, width)
    target_ids = jnp.arange(LAYERS, dtype=jnp.int32)
    target_slots = jnp.where((target_ids == source)[:, None, None], section_sum[None], 0.0)
    totals = lax.psum(target_slots, "layer")
    recon_sum = jnp.swapaxes(totals, 0, 1) + dec_bias[None]
    errors = (recon_sum - mlp_out.astype(jnp.float32)).astype(jnp.bfloat16)
    gathered = lax.all_gather(errors, ("feat", "row"), axis=0, tiled=True)
    error_grid = gathered.reshape(feat_count, row_count, rows_each, LAYERS, width)
    errors_mine = lax.dynamic_index_in_dim(error_grid, row_pos, axis=1, keepdims=False)
    errors_mine = errors_mine.reshape(local_rows, LAYERS, width)
    errors_half = lax.dynamic_slice_in_dim(
        jnp.swapaxes(error_grid, 0, 1), row_pos * half_width, half_width, axis=4
    )
    errors_half = errors_half.reshape(total_rows, LAYERS, half_width)
    live_next = source + 1 < LAYERS
    next_index = jnp.minimum(source + 1, LAYERS - 1)
    half_own = lax.dynamic_index_in_dim(errors_half, source, axis=1, keepdims=False)
    half_next = lax.dynamic_index_in_dim(errors_half, next_index, axis=1, keepdims=False)
    half_next = jnp.where(live_next, half_next, jnp.zeros_like(half_next))
    half_terms = dot_last(half_own, own_half_dec) + dot_last(half_next, next_half_dec)
    grad_feats = lax.psum(half_terms, "row") * loss_scale
    grad_all = jnp.where(pre_all > 0, grad_feats, 0.0).astype(jnp.bfloat16)
    grad_own = loss_scale * dot_first(features_all, half_own)
    grad_next = loss_scale * dot_first(features_all, half_next)
    enc_grad = dot_first(grad_all, inputs_half).astype(jnp.bfloat16)
    dec_grad = jnp.stack([grad_own, grad_next], axis=1).astype(jnp.bfloat16)
    bias_grad = jnp.sum(grad_all.astype(jnp.float32), axis=0)
    return (recon_sum.astype(jnp.bfloat16), enc_grad[None], dec_grad[None], bias_grad[None])

KC = 256
DC = 128
MESH = pl.DeviceIdType.MESH
VMEM_LIMIT = 67043328
BF = jnp.bfloat16


def pick(rows, cols, stride, offset):
    r = lax.broadcasted_iota(jnp.int32, (rows, cols), 0)
    c = lax.broadcasted_iota(jnp.int32, (rows, cols), 1)
    return (c == stride * r + offset).astype(BF)


def mm(left, right):
    return jnp.dot(left, right, preferred_element_type=jnp.float32)


def step_kernel(
    n, J, res, shuf, mlp, enc, dec, bias, dbias,
    feats, xs, errs, gpre, parts,
    enc_v, wv, raw, xsend, xg, mlpx, msend, pre_own, pre_send, pre_recv, fall,
    nsend, nrecv, facc, osend, rrecv, e0, e1, rc, rb, g_own, g_send, g_recv, gall,
    sem_l, sem_raw, x_s, x_r, m_s, m_r, p_s, p_r, f_s, f_r, n_s, n_r, r_s, r_r,
    e_s, e_r, t_s, t_r, b_s, b_r, g_s, g_r, q_s, q_r, y_s, w_s,
):
    z = lax.axis_index("feat")
    x = lax.axis_index("layer")
    c = lax.axis_index("row")
    R, H = xsend.shape[1:]
    F = enc_v.shape[0]
    T = xs.shape[0]
    T2, CR, NC = T // 2, 2 * R, H // J
    nk = F // KC
    scale = float(T) ** (-0.5)
    other_c, other_x = 1 - c, 1 - x

    def far(dz):
        return lax.rem(z + dz, n)

    def back(dz):
        return lax.rem(z + n - dz, n)

    def remote(src, dst, send, recv, **where):
        return pltpu.make_async_remote_copy(
            src_ref=src, dst_ref=dst, send_sem=send, recv_sem=recv,
            device_id=where, device_id_type=MESH)

    line = n == 4

    def unless_ends(dz, act):
        if line and dz == n - 1:
            pl.when(z != 0)(act)
        elif line and dz == 1:
            pl.when(z != n - 1)(act)
        else:
            act()

    def relays(act):
        if line:
            pl.when(z == 2)(lambda: act(1, 3))
            pl.when(z == 1)(lambda: act(3, 1))

    orders = (2, 1, 3) if line else tuple(range(1, n))

    enc_copy = pltpu.make_async_copy(enc, enc_v, sem_l)
    enc_copy.start()

    def raw_copy(i, slot):
        return pltpu.make_async_copy(
            dec.at[pl.ds(pl.multiple_of(i * DC, DC), DC)], raw.at[slot], sem_raw.at[slot])

    raw_copy(0, 0).start()

    barrier = pltpu.get_barrier_semaphore()
    for dz in range(n):
        if dz:
            pl.semaphore_signal(barrier, inc=1, device_id={"feat": far(dz), "row": c}, device_id_type=MESH)
        pl.semaphore_signal(barrier, inc=1, device_id={"feat": far(dz), "row": other_c}, device_id_type=MESH)
    for cc in (c, other_c):
        pl.semaphore_signal(barrier, inc=1, device_id={"layer": other_x, "row": cc}, device_id_type=MESH)

    own_x = mm(pick(R, 2 * R, 2, x), res.reshape(2 * R, 2 * H)[...]).astype(BF)
    x_mine = jnp.where(c == 0, own_x[:, :H], own_x[:, H:])
    xsend[0] = x_mine
    xsend[1] = jnp.where(c == 0, own_x[:, H:], own_x[:, :H])
    xg[z, c] = x_mine
    own_m = mm(pick(R, 2 * R, 2, x), mlp.reshape(2 * R, 2 * H)[...]).astype(BF)
    mlpx[c] = jnp.where(c == 0, own_m[:, :H], own_m[:, H:])
    msend[...] = jnp.where(c == 0, own_m[:, H:], own_m[:, :H])

    pl.semaphore_wait(barrier, 2 * n + 1)

    def x_copy(dz, k):
        return remote(xsend.at[k], xg.at[z, c], x_s.at[dz, k], x_r.at[dz, k],
                      feat=far(dz), row=c if k == 0 else other_c)

    x_list = [(dz, k) for dz in orders for k in range(2)] + [(0, 1)]
    for dz, k in x_list:
        unless_ends(dz, lambda: x_copy(dz, k).start())

    def y_copy(k, to, at):
        cc = c if k == 0 else other_c
        return remote(xg.at[back(2), cc], xg.at[back(2), cc], y_s.at[k], x_r.at[at, k], feat=far(to))

    m_copy = remote(msend, mlpx.at[c], m_s, m_r, row=other_c)
    m_copy.start()

    s0, s1 = pick(DC, 2 * DC, 2, 0), pick(DC, 2 * DC, 2, 1)
    nd = F // DC

    def split_body(i, carry):
        slot = lax.rem(i, 2)

        @pl.when(i + 1 < nd)
        def _():
            raw_copy(i + 1, 1 - slot).start()

        raw_copy(i, slot).wait()
        blk = raw.at[slot].reshape(2 * DC, H)[...]
        rows = pl.ds(pl.multiple_of(i * DC, DC), DC)
        wv[0, rows, :] = mm(s0, blk).astype(BF)
        wv[1, rows, :] = mm(s1, blk).astype(BF)
        return carry

    lax.fori_loop(0, nd // 2, split_body, 0)
    if line:
        for k in range(2):
            x_copy(2, k).wait_recv()
            relays(lambda to, at: y_copy(k, to, at).start())
    lax.fori_loop(nd // 2, nd, split_body, 0)

    for dz, k in x_list:
        if not line or dz != 2:
            x_copy(dz, k).wait_recv()
    perm = (lax.broadcasted_iota(jnp.int32, (T, T), 0) == shuf[...]).astype(BF)

    def perm_body(q, carry):
        cols = pl.ds(pl.multiple_of(q * KC, KC), KC)
        xs[:, cols] = dot_first(perm, xg[:, :, :, cols].reshape(T, KC)).astype(BF)
        return carry

    lax.fori_loop(0, H // KC, perm_body, 0)
    enc_copy.wait()

    def cols_of(k):
        return pl.ds(pl.multiple_of(k * KC, KC), KC)

    def keep_and_send(v, k, own, send):
        top, bot = v[:T2], v[T2:]
        own[k] = jnp.where(c == 0, top, bot)
        send[k] = jnp.where(c == 0, bot, top)

    def p_copy(k):
        return remote(pre_send.at[k], pre_recv.at[k], p_s.at[k], p_r.at[k], row=other_c)

    def f_copy(k):
        return remote(fall.at[c, k], fall.at[c, k], f_s.at[k], f_r.at[k], row=other_c)

    def pre_body(k, carry):
        keep_and_send(dot_last(xs[...], enc_v[cols_of(k), :]), k, pre_own, pre_send)
        p_copy(k).start()
        return carry

    lax.fori_loop(0, nk, pre_body, 0)

    def feat_body(k, carry):
        p_copy(k).wait_recv()
        v = pre_own[k] + pre_recv[k] + bias[:, cols_of(k)]
        fall[c, k] = jnp.maximum(v, 0.0).astype(BF)
        f_copy(k).start()
        return carry

    lax.fori_loop(0, nk, feat_body, 0)

    def join_body(k, carry):
        f_copy(k).wait_recv()
        feats[:, cols_of(k)] = jnp.concatenate([fall[0, k], fall[1, k]], axis=0)
        return carry

    lax.fori_loop(0, nk, join_body, 0)

    def n_copy(j):
        return remote(nsend.at[j], nrecv.at[j], n_s.at[j], n_r.at[j], layer=other_x)

    def r_copy(j, dz):
        return remote(osend.at[j, far(dz)], rrecv.at[j, dz - 1], r_s.at[j, dz], r_r.at[j, dz], feat=far(dz))

    def e_copy(j, dz):
        return remote(e0.at[j, z], e0.at[j, z], e_s.at[j, dz], e_r.at[j, dz], feat=far(dz))

    def w_copy(j, to, at):
        return remote(e0.at[j, back(2)], e0.at[j, back(2)], w_s.at[j], e_r.at[j, at], feat=far(to))

    def t_copy(j, dz):
        return remote(e0.at[j, back(dz)], e1.at[j, back(dz)], t_s.at[j, dz], t_r.at[j, dz], layer=other_x)

    def spots(j, q):
        wide = pl.ds(pl.multiple_of(j * NC + q * KC, KC), KC)
        return wide, pl.ds(pl.multiple_of(q * KC, KC), KC)

    @pl.when(x == 0)
    def _():
        for j in range(J):
            def next_body(q, carry):
                wide, near = spots(j, q)
                nsend[j, :, near] = mm(feats[...], wv[1, :, wide]).astype(BF)
                return carry

            lax.fori_loop(0, NC // KC, next_body, 0)
            n_copy(j).start()

            def own_body(q, carry):
                wide, near = spots(j, q)
                v = mm(feats[...], wv[0, :, wide]).reshape(n, CR, KC)
                facc[:, :, wide] = v
                osend[j, :, :, near] = v.astype(BF)
                return carry

            lax.fori_loop(0, NC // KC, own_body, 0)
            for dz in range(1, n):
                r_copy(j, dz).start()

    @pl.when(x == 1)
    def _():
        for j in range(J):
            def own_body(q, carry):
                wide, near = spots(j, q)
                facc[:, :, wide] = mm(feats[...], wv[0, :, wide]).reshape(n, CR, KC)
                return carry

            lax.fori_loop(0, NC // KC, own_body, 0)
        for j in range(J):
            n_copy(j).wait_recv()

            def add_body(q, carry):
                wide, near = spots(j, q)
                v = facc[:, :, wide] + nrecv[j, :, near].astype(jnp.float32).reshape(n, CR, KC)
                facc[:, :, wide] = v
                osend[j, :, :, near] = v.astype(BF)
                return carry

            lax.fori_loop(0, NC // KC, add_body, 0)
            for dz in range(1, n):
                r_copy(j, dz).start()

    m_copy.wait_recv()

    def reduce_chunk(j):
        for dz in range(1, n):
            r_copy(j, dz).wait_recv()
        wide = pl.ds(j * NC, NC)
        total = facc[z, :, wide]
        for dz in range(1, n):
            total = total + rrecv[j, dz - 1].astype(jnp.float32)
        d = jnp.where(
            x == 0,
            jnp.where(c == 0, dbias[0:1, j * NC:(j + 1) * NC], dbias[0:1, H + j * NC:H + (j + 1) * NC]),
            jnp.where(c == 0, dbias[1:2, j * NC:(j + 1) * NC], dbias[1:2, H + j * NC:H + (j + 1) * NC]))
        total = total + d
        e0[j, z] = (total - mlpx[:, :, wide].reshape(CR, NC).astype(jnp.float32)).astype(BF)
        for dz in orders:
            unless_ends(dz, lambda: e_copy(j, dz).start())

        @pl.when(x == 1)
        def _():
            t_copy(j, 0).start()

        rc[:, j] = total.astype(BF).reshape(2, R, NC)

    def pass_chunk(j):
        for dz in orders:
            e_copy(j, dz).wait_recv()
            if line and dz == 2:
                relays(lambda to, at: w_copy(j, to, at).start())

            @pl.when(x == 1)
            def _():
                t_copy(j, dz).start()

    for j in range(J):
        reduce_chunk(j)
        if j:
            pass_chunk(j - 1)
    pass_chunk(J - 1)

    def b_copy(k):
        dx, dc = k // 2, k % 2
        to_x = other_x if dx else x
        to_c = other_c if dc else c
        return remote(rc.at[to_c], rb.at[x, c], b_s.at[k], b_r.at[k], layer=to_x, row=to_c)

    for k in range(1, 4):
        b_copy(k).start()
    rb[x, c] = rc[c]

    for j in range(J):
        errs[0, :, j * NC:(j + 1) * NC] = e0[j].reshape(T, NC)

    @pl.when(x == 0)
    def _():
        for j in range(J):
            for dz in range(n):
                t_copy(j, dz).wait_recv()
            errs[1, :, j * NC:(j + 1) * NC] = e1[j].reshape(T, NC)

    @pl.when(x == 1)
    def _():
        errs[1] = jnp.zeros((T, H), BF)

    def g_copy(k):
        return remote(g_send.at[k], g_recv.at[k], g_s.at[k], g_r.at[k], row=other_c)

    def q_copy(k):
        return remote(gall.at[c, k], gall.at[c, k], q_s.at[k], q_r.at[k], row=other_c)

    @pl.when(x == 0)
    def _():
        def grad_body(k, carry):
            v = dot_last(errs[0], wv[0, cols_of(k), :]) + dot_last(errs[1], wv[1, cols_of(k), :])
            keep_and_send(v, k, g_own, g_send)
            g_copy(k).start()
            return carry

        lax.fori_loop(0, nk, grad_body, 0)

    @pl.when(x == 1)
    def _():
        def grad_body(k, carry):
            keep_and_send(dot_last(errs[0], wv[0, cols_of(k), :]), k, g_own, g_send)
            g_copy(k).start()
            return carry

        lax.fori_loop(0, nk, grad_body, 0)

    def mask_body(k, carry):
        g_copy(k).wait_recv()
        v = (g_own[k] + g_recv[k]) * scale
        gall[c, k] = jnp.where(fall[c, k].astype(jnp.float32) > 0, v, 0.0).astype(BF)
        q_copy(k).start()
        return carry

    lax.fori_loop(0, nk, mask_body, 0)

    for k in range(1, 4):
        b_copy(k).wait_recv()
    for h in range(2):
        for j in range(J):
            lo = h * H + j * NC
            parts[:, lo:lo + NC] = rb[:, h, j].reshape(2 * R, NC)

    def last_body(k, carry):
        q_copy(k).wait_recv()
        both = jnp.concatenate([gall[0, k], gall[1, k]], axis=0)
        gpre[:, cols_of(k)] = both
        p_copy(k).wait_send()
        f_copy(k).wait_send()
        g_copy(k).wait_send()
        q_copy(k).wait_send()
        return carry

    lax.fori_loop(0, nk, last_body, 0)

    for dz, k in x_list:
        unless_ends(dz, lambda: x_copy(dz, k).wait_send())
    for k in range(2):
        relays(lambda to, at: y_copy(k, to, at).wait_send())
    for j in range(J):
        relays(lambda to, at: w_copy(j, to, at).wait_send())
    m_copy.wait_send()
    for j in range(J):
        for dz in range(1, n):
            r_copy(j, dz).wait_send()
            unless_ends(dz, lambda: e_copy(j, dz).wait_send())
    for k in range(1, 4):
        b_copy(k).wait_send()

    @pl.when(x == 0)
    def _():
        for j in range(J):
            n_copy(j).wait_send()

    @pl.when(x == 1)
    def _():
        for j in range(J):
            for dz in range(n):
                t_copy(j, dz).wait_send()


def weight_kernel(scale, feats, gpre, errs, xs, parts, enc_grad, dec_grad, bgrad, rebuilt):
    fc, H = enc_grad.shape
    R2 = parts.shape[0]

    @pl.when(pl.program_id(0) == 0)
    def _():
        i = lax.broadcasted_iota(jnp.int32, (R2, R2), 0)
        j = lax.broadcasted_iota(jnp.int32, (R2, R2), 1)
        inter = (j == (i % 2) * (R2 // 2) + i // 2).astype(BF)
        rebuilt.reshape(R2, 2 * H)[...] = mm(inter, parts[...]).astype(BF)

    bgrad[...] = jnp.sum(gpre[...].astype(jnp.float32), axis=0, keepdims=True)
    enc_grad[...] = dot_first(gpre[...], xs[...]).astype(BF)
    p0, p1 = pick(DC, 2 * DC, 2, 0), pick(DC, 2 * DC, 2, 1)
    out = dec_grad.reshape(2 * fc, H)
    for b in range(fc // DC):
        f = feats[:, b * DC:(b + 1) * DC]
        g = dot_first(mm(f, p0).astype(BF), errs[0]) + dot_first(mm(f, p1).astype(BF), errs[1])
        out[b * 2 * DC:(b + 1) * 2 * DC, :] = (scale * g).astype(BF)


def fused(resid_buf, shuffle, mlp_out, enc_weight, dec_weight, enc_bias, dec_bias):
    n = lax.axis_size("feat")
    R = resid_buf.shape[0]
    F, H = enc_weight.shape[1:]
    T = R * n * 2
    T2, CR = T // 2, 2 * R
    J = H // KC
    NC, nk = H // J, F // KC
    f32 = jnp.float32
    vm = pl.BlockSpec(memory_space=pltpu.VMEM)
    hbm = pl.BlockSpec(memory_space=pl.ANY)
    dma = pltpu.SemaphoreType.DMA
    shape = jax.ShapeDtypeStruct
    feats, xs, errs, gpre, parts = pl.pallas_call(
        functools.partial(step_kernel, n, J),
        out_shape=(
            shape((T, F), BF), shape((T, H), BF), shape((2, T, H), BF), shape((T, F), BF),
            shape((2 * R, 2 * H), BF)),
        in_specs=[vm, vm, vm, hbm, hbm, vm, vm],
        out_specs=[vm] * 5,
        scratch_shapes=[
            pltpu.VMEM((F, H), BF), pltpu.VMEM((2, F, H), BF), pltpu.VMEM((2, DC, 2, H), BF),
            pltpu.VMEM((2, R, H), BF), pltpu.VMEM((n, 2, R, H), BF),
            pltpu.VMEM((2, R, H), BF), pltpu.VMEM((R, H), BF),
            pltpu.VMEM((nk, T2, KC), f32), pltpu.VMEM((nk, T2, KC), f32), pltpu.VMEM((nk, T2, KC), f32),
            pltpu.VMEM((2, nk, T2, KC), BF),
            pltpu.VMEM((J, T, NC), BF), pltpu.VMEM((J, T, NC), BF), pltpu.VMEM((n, CR, H), f32),
            pltpu.VMEM((J, n, CR, NC), BF), pltpu.VMEM((J, n - 1, CR, NC), BF),
            pltpu.VMEM((J, n, CR, NC), BF), pltpu.VMEM((J, n, CR, NC), BF),
            pltpu.VMEM((2, J, R, NC), BF), pltpu.VMEM((2, 2, J, R, NC), BF),
            pltpu.VMEM((nk, T2, KC), f32), pltpu.VMEM((nk, T2, KC), f32), pltpu.VMEM((nk, T2, KC), f32),
            pltpu.VMEM((2, nk, T2, KC), BF),
            dma, dma((2,)), dma((n, 2)), dma((n, 2)), dma, dma, dma((nk,)), dma((nk,)),
            dma((nk,)), dma((nk,)), dma((J,)), dma((J,)), dma((J, n)), dma((J, n)),
            dma((J, n)), dma((J, n)), dma((J, n)), dma((J, n)), dma((4,)), dma((4,)),
            dma((nk,)), dma((nk,)), dma((nk,)), dma((nk,)), dma((2,)), dma((J,)),
        ],
        compiler_params=pltpu.CompilerParams(
            collective_id=0, has_side_effects=True, vmem_limit_bytes=VMEM_LIMIT),
    )(resid_buf, shuffle.reshape(1, T), mlp_out, enc_weight[0], dec_weight[0], enc_bias, dec_bias)
    fc = 512 if F % 512 == 0 else KC
    enc_grad, dec_grad, bgrad, rebuilt = pl.pallas_call(
        functools.partial(weight_kernel, float(T) ** (-0.5)),
        grid=(F // fc,),
        out_shape=(
            shape((F, H), BF), shape((F, 2, H), BF), shape((1, F), f32), shape((R, 2, 2 * H), BF)),
        in_specs=[
            pl.BlockSpec((T, fc), lambda i: (0, i)), pl.BlockSpec((T, fc), lambda i: (0, i)),
            pl.BlockSpec((2, T, H), lambda i: (0, 0, 0)), pl.BlockSpec((T, H), lambda i: (0, 0)),
            pl.BlockSpec((2 * R, 2 * H), lambda i: (0, 0))],
        out_specs=(
            pl.BlockSpec((fc, H), lambda i: (i, 0)), pl.BlockSpec((fc, 2, H), lambda i: (i, 0, 0)),
            pl.BlockSpec((1, fc), lambda i: (0, i)), pl.BlockSpec((R, 2, 2 * H), lambda i: (0, 0, 0))),
        compiler_params=pltpu.CompilerParams(vmem_limit_bytes=VMEM_LIMIT),
    )(feats, gpre, errs, xs, parts)
    return rebuilt, enc_grad[None], dec_grad[None], bgrad


def chosen(resid_buf, shuffle, mlp_out, enc_weight, dec_weight, enc_bias, dec_bias):
    args = (resid_buf, shuffle, mlp_out, enc_weight, dec_weight, enc_bias, dec_bias)
    rows, width = resid_buf.shape[0], enc_weight.shape[2]
    fits = (
        lax.axis_size("layer") == LAYERS == 2 and lax.axis_size("row") == 2
        and 1 < lax.axis_size("feat") <= 4 and rows % 16 == 0
        and width % KC == 0 and enc_weight.shape[1] % KC == 0)
    return fused(*args) if fits else on_device(*args)


def solution(mesh):
    return jax.shard_map(
        chosen,
        mesh=mesh,
        in_specs=(
            P(("groups", "feat", "row"), None, None),
            P("groups"),
            P(("groups", "feat", "row"), None, None),
            P("layer", "feat", "row"),
            P("layer", "feat", None, "row"),
            P("layer", "feat"),
            P(),
        ),
        out_specs=(
            P(("groups", "feat", "row"), None, None),
            P(("groups", "layer"), "feat", "row"),
            P(("groups", "layer"), "feat", None, "row"),
            P(("groups", "layer"), "feat"),
        ),
        check_vma=False,
    )
```

```python
import functools

import jax
import jax.numpy as jnp
from jax import lax
from jax.experimental import pallas as pl
from jax.experimental.pallas import tpu as pltpu
from jax.sharding import PartitionSpec as P

LAYERS = 2


def from_behind(block, axis, distance):
    devices = range(lax.axis_size(axis))
    route = [(i - distance, i) for i in devices if i - distance in devices]
    return lax.ppermute(block, axis, route)


def dot_last(left, right):
    return lax.dot_general(
        left, right, (((1,), (1,)), ((), ())), preferred_element_type=jnp.float32
    )


def dot_first(left, right):
    return lax.dot_general(
        left, right, (((0,), (0,)), ((), ())), preferred_element_type=jnp.float32
    )


def on_device(resid_buf, shuffle, mlp_out, enc_weight, dec_weight, enc_bias, dec_bias):
    feat_count = lax.axis_size("feat")
    row_count = lax.axis_size("row")
    sub_blocks = lax.axis_size("layer") // LAYERS
    layer_pos = lax.axis_index("layer")
    row_pos = lax.axis_index("row")
    source = layer_pos // sub_blocks
    rows_each = resid_buf.shape[0]
    width = dec_bias.shape[1]
    half_width = enc_weight.shape[2]
    local_rows = rows_each * feat_count
    total_rows = local_rows * row_count
    loss_scale = float(total_rows) ** (-0.5)
    own_layer = lax.dynamic_index_in_dim(resid_buf, source, axis=1, keepdims=False)
    buffer_all = lax.all_gather(own_layer, ("feat", "row"), axis=0, tiled=True)
    batch_rows = jnp.take(buffer_all, shuffle, axis=0)
    blocks = batch_rows.reshape(feat_count, row_count, rows_each, width)
    inputs_half = lax.dynamic_slice_in_dim(
        jnp.swapaxes(blocks, 0, 1), row_pos * half_width, half_width, axis=3
    )
    inputs_half = inputs_half.reshape(total_rows, half_width)
    own_half_dec = dec_weight[0][:, 0]
    next_half_dec = dec_weight[0][:, 1]
    pre_all = lax.psum(dot_last(inputs_half, enc_weight[0]), "row") + enc_bias[0]
    features_all = jnp.maximum(pre_all, 0.0).astype(jnp.bfloat16)
    own_part = jnp.dot(features_all, own_half_dec, preferred_element_type=jnp.float32)
    next_part = jnp.dot(features_all, next_half_dec, preferred_element_type=jnp.float32)
    carried = from_behind(next_part, "layer", sub_blocks)
    spread = (own_part + carried).reshape(row_count, local_rows, half_width)
    halves = lax.psum_scatter(spread, "feat", scatter_dimension=1, tiled=True)
    joined = lax.all_to_all(halves, "row", split_axis=0, concat_axis=2, tiled=True)
    section_sum = joined.reshape(rows_each, width)
    target_ids = jnp.arange(LAYERS, dtype=jnp.int32)
    target_slots = jnp.where((target_ids == source)[:, None, None], section_sum[None], 0.0)
    totals = lax.psum(target_slots, "layer")
    recon_sum = jnp.swapaxes(totals, 0, 1) + dec_bias[None]
    errors = (recon_sum - mlp_out.astype(jnp.float32)).astype(jnp.bfloat16)
    gathered = lax.all_gather(errors, ("feat", "row"), axis=0, tiled=True)
    error_grid = gathered.reshape(feat_count, row_count, rows_each, LAYERS, width)
    errors_mine = lax.dynamic_index_in_dim(error_grid, row_pos, axis=1, keepdims=False)
    errors_mine = errors_mine.reshape(local_rows, LAYERS, width)
    errors_half = lax.dynamic_slice_in_dim(
        jnp.swapaxes(error_grid, 0, 1), row_pos * half_width, half_width, axis=4
    )
    errors_half = errors_half.reshape(total_rows, LAYERS, half_width)
    live_next = source + 1 < LAYERS
    next_index = jnp.minimum(source + 1, LAYERS - 1)
    half_own = lax.dynamic_index_in_dim(errors_half, source, axis=1, keepdims=False)
    half_next = lax.dynamic_index_in_dim(errors_half, next_index, axis=1, keepdims=False)
    half_next = jnp.where(live_next, half_next, jnp.zeros_like(half_next))
    half_terms = dot_last(half_own, own_half_dec) + dot_last(half_next, next_half_dec)
    grad_feats = lax.psum(half_terms, "row") * loss_scale
    grad_all = jnp.where(pre_all > 0, grad_feats, 0.0).astype(jnp.bfloat16)
    grad_own = loss_scale * dot_first(features_all, half_own)
    grad_next = loss_scale * dot_first(features_all, half_next)
    enc_grad = dot_first(grad_all, inputs_half).astype(jnp.bfloat16)
    dec_grad = jnp.stack([grad_own, grad_next], axis=1).astype(jnp.bfloat16)
    bias_grad = jnp.sum(grad_all.astype(jnp.float32), axis=0)
    return (recon_sum.astype(jnp.bfloat16), enc_grad[None], dec_grad[None], bias_grad[None])

KC = 256
DC = 128
MESH = pl.DeviceIdType.MESH
VMEM_LIMIT = 67043328
BF = jnp.bfloat16


def pick(rows, cols, stride, offset):
    r = lax.broadcasted_iota(jnp.int32, (rows, cols), 0)
    c = lax.broadcasted_iota(jnp.int32, (rows, cols), 1)
    return (c == stride * r + offset).astype(BF)


def mm(left, right):
    return jnp.dot(left, right, preferred_element_type=jnp.float32)


def step_kernel(
    n, J, res, shuf, mlp, enc, dec, bias, dbias,
    feats, xs, errs, gpre, parts,
    enc_v, wv, raw, xsend, xg, mlpx, msend, pre_own, pre_send, pre_recv, fall,
    nsend, nrecv, facc, osend, rrecv, e0, e1, rc, rb, g_own, g_send, g_recv, gall,
    sem_l, sem_raw, x_s, x_r, m_s, m_r, p_s, p_r, f_s, f_r, n_s, n_r, r_s, r_r,
    e_s, e_r, t_s, t_r, b_s, b_r, g_s, g_r, q_s, q_r, y_s, w_s,
):
    z = lax.axis_index("feat")
    x = lax.axis_index("layer")
    c = lax.axis_index("row")
    R, H = xsend.shape[1:]
    F = enc_v.shape[0]
    T = xs.shape[0]
    T2, CR, NC = T // 2, 2 * R, H // J
    nk = F // KC
    scale = float(T) ** (-0.5)
    other_c, other_x = 1 - c, 1 - x

    def far(dz):
        return lax.rem(z + dz, n)

    def back(dz):
        return lax.rem(z + n - dz, n)

    def remote(src, dst, send, recv, **where):
        return pltpu.make_async_remote_copy(
            src_ref=src, dst_ref=dst, send_sem=send, recv_sem=recv,
            device_id=where, device_id_type=MESH)

    line = n == 4

    def unless_ends(dz, act):
        if line and dz == n - 1:
            pl.when(z != 0)(act)
        elif line and dz == 1:
            pl.when(z != n - 1)(act)
        else:
            act()

    def relays(act):
        if line:
            pl.when(z == 2)(lambda: act(1, 3))
            pl.when(z == 1)(lambda: act(3, 1))

    orders = (2, 1, 3) if line else tuple(range(1, n))

    enc_copy = pltpu.make_async_copy(enc, enc_v, sem_l)
    enc_copy.start()

    def raw_copy(i, slot):
        return pltpu.make_async_copy(
            dec.reshape(2 * F, H).at[pl.ds(pl.multiple_of(i * 2 * DC, 2 * DC), 2 * DC)], raw.at[slot], sem_raw.at[slot])

    raw_copy(0, 0).start()

    barrier = pltpu.get_barrier_semaphore()
    for dz in range(n):
        if dz:
            pl.semaphore_signal(barrier, inc=1, device_id={"feat": far(dz), "row": c}, device_id_type=MESH)
        pl.semaphore_signal(barrier, inc=1, device_id={"feat": far(dz), "row": other_c}, device_id_type=MESH)
    for cc in (c, other_c):
        pl.semaphore_signal(barrier, inc=1, device_id={"layer": other_x, "row": cc}, device_id_type=MESH)

    own_x = mm(pick(R, 2 * R, 2, x), res.reshape(2 * R, 2 * H)[...]).astype(BF)
    x_mine = jnp.where(c == 0, own_x[:, :H], own_x[:, H:])
    xsend[0] = x_mine
    xsend[1] = jnp.where(c == 0, own_x[:, H:], own_x[:, :H])
    xg[z, c] = x_mine
    own_m = mm(pick(R, 2 * R, 2, x), mlp.reshape(2 * R, 2 * H)[...]).astype(BF)
    mlpx[c] = jnp.where(c == 0, own_m[:, :H], own_m[:, H:])
    msend[...] = jnp.where(c == 0, own_m[:, H:], own_m[:, :H])

    pl.semaphore_wait(barrier, 2 * n + 1)

    def x_copy(dz, k):
        return remote(xsend.at[k], xg.at[z, c], x_s.at[dz, k], x_r.at[dz, k],
                      feat=far(dz), row=c if k == 0 else other_c)

    x_list = [(dz, k) for dz in orders for k in range(2)] + [(0, 1)]
    for dz, k in x_list:
        unless_ends(dz, lambda: x_copy(dz, k).start())

    def y_copy(k, to, at):
        cc = c if k == 0 else other_c
        return remote(xg.at[back(2), cc], xg.at[back(2), cc], y_s.at[k], x_r.at[at, k], feat=far(to))

    m_copy = remote(msend, mlpx.at[c], m_s, m_r, row=other_c)
    m_copy.start()

    apart = jnp.concatenate([pick(DC, 2 * DC, 2, 0), pick(DC, 2 * DC, 2, 1)], axis=0)
    nd = F // DC

    def split_body(i, carry):
        slot = lax.rem(i, 2)

        @pl.when(i + 1 < nd)
        def _():
            raw_copy(i + 1, 1 - slot).start()

        raw_copy(i, slot).wait()
        both = mm(apart, raw[slot]).astype(BF)
        rows = pl.ds(pl.multiple_of(i * DC, DC), DC)
        wv[0, rows, :] = both[:DC]
        wv[1, rows, :] = both[DC:]
        return carry

    lax.fori_loop(0, nd // 2, split_body, 0)
    if line:
        for k in range(2):
            x_copy(2, k).wait_recv()
            relays(lambda to, at: y_copy(k, to, at).start())
    lax.fori_loop(nd // 2, nd, split_body, 0)

    for dz, k in x_list:
        if not line or dz != 2:
            x_copy(dz, k).wait_recv()
    perm = (lax.broadcasted_iota(jnp.int32, (T, T), 0) == shuf[...]).astype(BF)

    def perm_body(q, carry):
        cols = pl.ds(pl.multiple_of(q * KC, KC), KC)
        xs[:, cols] = dot_first(perm, xg[:, :, :, cols].reshape(T, KC)).astype(BF)
        return carry

    lax.fori_loop(0, H // KC, perm_body, 0)
    enc_copy.wait()

    def cols_of(k):
        return pl.ds(pl.multiple_of(k * KC, KC), KC)

    def keep_and_send(v, k, own, send):
        top, bot = v[:T2], v[T2:]
        own[k] = jnp.where(c == 0, top, bot)
        send[k] = jnp.where(c == 0, bot, top)

    def p_copy(k):
        return remote(pre_send.at[k], pre_recv.at[k], p_s.at[k], p_r.at[k], row=other_c)

    def f_copy(k):
        return remote(fall.at[c, k], fall.at[c, k], f_s.at[k], f_r.at[k], row=other_c)

    def pre_body(k, carry):
        keep_and_send(dot_last(xs[...], enc_v[cols_of(k), :]), k, pre_own, pre_send)
        p_copy(k).start()
        return carry

    lax.fori_loop(0, nk, pre_body, 0)

    def feat_body(k, carry):
        p_copy(k).wait_recv()
        v = pre_own[k] + pre_recv[k] + bias[:, cols_of(k)]
        fall[c, k] = jnp.maximum(v, 0.0).astype(BF)
        f_copy(k).start()
        return carry

    lax.fori_loop(0, nk, feat_body, 0)

    def join_body(k, carry):
        f_copy(k).wait_recv()
        feats[:, cols_of(k)] = jnp.concatenate([fall[0, k], fall[1, k]], axis=0)
        return carry

    lax.fori_loop(0, nk, join_body, 0)

    def n_copy(j):
        return remote(nsend.at[j], nrecv.at[j], n_s.at[j], n_r.at[j], layer=other_x)

    def r_copy(j, dz):
        return remote(osend.at[j, far(dz)], rrecv.at[j, dz - 1], r_s.at[j, dz], r_r.at[j, dz], feat=far(dz))

    def e_copy(j, dz):
        return remote(e0.at[j, z], e0.at[j, z], e_s.at[j, dz], e_r.at[j, dz], feat=far(dz))

    def w_copy(j, to, at):
        return remote(e0.at[j, back(2)], e0.at[j, back(2)], w_s.at[j], e_r.at[j, at], feat=far(to))

    def t_copy(j, dz):
        return remote(e0.at[j, back(dz)], e1.at[j, back(dz)], t_s.at[j, dz], t_r.at[j, dz], layer=other_x)

    def spots(j, q):
        wide = pl.ds(pl.multiple_of(j * NC + q * KC, KC), KC)
        return wide, pl.ds(pl.multiple_of(q * KC, KC), KC)

    @pl.when(x == 0)
    def _():
        for j in range(J):
            def next_body(q, carry):
                wide, near = spots(j, q)
                nsend[j, :, near] = mm(feats[...], wv[1, :, wide]).astype(BF)
                return carry

            lax.fori_loop(0, NC // KC, next_body, 0)
            n_copy(j).start()

            def own_body(q, carry):
                wide, near = spots(j, q)
                v = mm(feats[...], wv[0, :, wide]).reshape(n, CR, KC)
                facc[:, :, wide] = v
                osend[j, :, :, near] = v.astype(BF)
                return carry

            lax.fori_loop(0, NC // KC, own_body, 0)
            for dz in range(1, n):
                r_copy(j, dz).start()

    @pl.when(x == 1)
    def _():
        for j in range(J):
            def own_body(q, carry):
                wide, near = spots(j, q)
                facc[:, :, wide] = mm(feats[...], wv[0, :, wide]).reshape(n, CR, KC)
                return carry

            lax.fori_loop(0, NC // KC, own_body, 0)
        for j in range(J):
            n_copy(j).wait_recv()

            def add_body(q, carry):
                wide, near = spots(j, q)
                v = facc[:, :, wide] + nrecv[j, :, near].astype(jnp.float32).reshape(n, CR, KC)
                facc[:, :, wide] = v
                osend[j, :, :, near] = v.astype(BF)
                return carry

            lax.fori_loop(0, NC // KC, add_body, 0)
            for dz in range(1, n):
                r_copy(j, dz).start()

    m_copy.wait_recv()

    def reduce_chunk(j):
        for dz in range(1, n):
            r_copy(j, dz).wait_recv()
        wide = pl.ds(j * NC, NC)
        total = facc[z, :, wide]
        for dz in range(1, n):
            total = total + rrecv[j, dz - 1].astype(jnp.float32)
        d = jnp.where(
            x == 0,
            jnp.where(c == 0, dbias[0:1, j * NC:(j + 1) * NC], dbias[0:1, H + j * NC:H + (j + 1) * NC]),
            jnp.where(c == 0, dbias[1:2, j * NC:(j + 1) * NC], dbias[1:2, H + j * NC:H + (j + 1) * NC]))
        total = total + d
        e0[j, z] = (total - mlpx[:, :, wide].reshape(CR, NC).astype(jnp.float32)).astype(BF)
        for dz in orders:
            unless_ends(dz, lambda: e_copy(j, dz).start())

        @pl.when(x == 1)
        def _():
            t_copy(j, 0).start()

        rc[:, j] = total.astype(BF).reshape(2, R, NC)

    def pass_chunk(j):
        for dz in orders:
            e_copy(j, dz).wait_recv()
            if line and dz == 2:
                relays(lambda to, at: w_copy(j, to, at).start())

            @pl.when(x == 1)
            def _():
                t_copy(j, dz).start()

    for j in range(J):
        reduce_chunk(j)
        if j:
            pass_chunk(j - 1)
    pass_chunk(J - 1)

    def b_copy(k):
        dx, dc = k // 2, k % 2
        to_x = other_x if dx else x
        to_c = other_c if dc else c
        return remote(rc.at[to_c], rb.at[x, c], b_s.at[k], b_r.at[k], layer=to_x, row=to_c)

    for k in range(1, 4):
        b_copy(k).start()
    rb[x, c] = rc[c]

    for j in range(J):
        errs[0, :, j * NC:(j + 1) * NC] = e0[j].reshape(T, NC)

    @pl.when(x == 0)
    def _():
        for j in range(J):
            for dz in range(n):
                t_copy(j, dz).wait_recv()
            errs[1, :, j * NC:(j + 1) * NC] = e1[j].reshape(T, NC)

    @pl.when(x == 1)
    def _():
        errs[1] = jnp.zeros((T, H), BF)

    def g_copy(k):
        return remote(g_send.at[k], g_recv.at[k], g_s.at[k], g_r.at[k], row=other_c)

    def q_copy(k):
        return remote(gall.at[c, k], gall.at[c, k], q_s.at[k], q_r.at[k], row=other_c)

    @pl.when(x == 0)
    def _():
        def grad_body(k, carry):
            v = dot_last(errs[0], wv[0, cols_of(k), :]) + dot_last(errs[1], wv[1, cols_of(k), :])
            keep_and_send(v, k, g_own, g_send)
            g_copy(k).start()
            return carry

        lax.fori_loop(0, nk, grad_body, 0)

    @pl.when(x == 1)
    def _():
        def grad_body(k, carry):
            keep_and_send(dot_last(errs[0], wv[0, cols_of(k), :]), k, g_own, g_send)
            g_copy(k).start()
            return carry

        lax.fori_loop(0, nk, grad_body, 0)

    def mask_body(k, carry):
        g_copy(k).wait_recv()
        v = (g_own[k] + g_recv[k]) * scale
        gall[c, k] = jnp.where(fall[c, k].astype(jnp.float32) > 0, v, 0.0).astype(BF)
        q_copy(k).start()
        return carry

    lax.fori_loop(0, nk, mask_body, 0)

    for k in range(1, 4):
        b_copy(k).wait_recv()
    for h in range(2):
        for j in range(J):
            lo = h * H + j * NC
            parts[:, lo:lo + NC] = rb[:, h, j].reshape(2 * R, NC)

    def last_body(k, carry):
        q_copy(k).wait_recv()
        both = jnp.concatenate([gall[0, k], gall[1, k]], axis=0)
        gpre[:, cols_of(k)] = both
        p_copy(k).wait_send()
        f_copy(k).wait_send()
        g_copy(k).wait_send()
        q_copy(k).wait_send()
        return carry

    lax.fori_loop(0, nk, last_body, 0)

    for dz, k in x_list:
        unless_ends(dz, lambda: x_copy(dz, k).wait_send())
    for k in range(2):
        relays(lambda to, at: y_copy(k, to, at).wait_send())
    for j in range(J):
        relays(lambda to, at: w_copy(j, to, at).wait_send())
    m_copy.wait_send()
    for j in range(J):
        for dz in range(1, n):
            r_copy(j, dz).wait_send()
            unless_ends(dz, lambda: e_copy(j, dz).wait_send())
    for k in range(1, 4):
        b_copy(k).wait_send()

    @pl.when(x == 0)
    def _():
        for j in range(J):
            n_copy(j).wait_send()

    @pl.when(x == 1)
    def _():
        for j in range(J):
            for dz in range(n):
                t_copy(j, dz).wait_send()


def weight_kernel(scale, feats, gpre, errs, xs, parts, enc_grad, dec_grad, bgrad, rebuilt):
    fc, H = enc_grad.shape
    R2 = parts.shape[0]

    @pl.when(pl.program_id(0) == 0)
    def _():
        i = lax.broadcasted_iota(jnp.int32, (R2, R2), 0)
        j = lax.broadcasted_iota(jnp.int32, (R2, R2), 1)
        inter = (j == (i % 2) * (R2 // 2) + i // 2).astype(BF)
        rebuilt.reshape(R2, 2 * H)[...] = mm(inter, parts[...]).astype(BF)

    bgrad[...] = jnp.sum(gpre[...].astype(jnp.float32), axis=0, keepdims=True)
    enc_grad[...] = dot_first(gpre[...], xs[...]).astype(BF)
    p0, p1 = pick(DC, 2 * DC, 2, 0), pick(DC, 2 * DC, 2, 1)
    out = dec_grad.reshape(2 * fc, H)
    for b in range(fc // DC):
        f = feats[:, b * DC:(b + 1) * DC]
        g = dot_first(mm(f, p0).astype(BF), errs[0]) + dot_first(mm(f, p1).astype(BF), errs[1])
        out[b * 2 * DC:(b + 1) * 2 * DC, :] = (scale * g).astype(BF)


def fused(resid_buf, shuffle, mlp_out, enc_weight, dec_weight, enc_bias, dec_bias):
    n = lax.axis_size("feat")
    R = resid_buf.shape[0]
    F, H = enc_weight.shape[1:]
    T = R * n * 2
    T2, CR = T // 2, 2 * R
    J = H // KC
    NC, nk = H // J, F // KC
    f32 = jnp.float32
    vm = pl.BlockSpec(memory_space=pltpu.VMEM)
    hbm = pl.BlockSpec(memory_space=pl.ANY)
    dma = pltpu.SemaphoreType.DMA
    shape = jax.ShapeDtypeStruct
    feats, xs, errs, gpre, parts = pl.pallas_call(
        functools.partial(step_kernel, n, J),
        out_shape=(
            shape((T, F), BF), shape((T, H), BF), shape((2, T, H), BF), shape((T, F), BF),
            shape((2 * R, 2 * H), BF)),
        in_specs=[vm, vm, vm, hbm, hbm, vm, vm],
        out_specs=[vm] * 5,
        scratch_shapes=[
            pltpu.VMEM((F, H), BF), pltpu.VMEM((2, F, H), BF), pltpu.VMEM((2, 2 * DC, H), BF),
            pltpu.VMEM((2, R, H), BF), pltpu.VMEM((n, 2, R, H), BF),
            pltpu.VMEM((2, R, H), BF), pltpu.VMEM((R, H), BF),
            pltpu.VMEM((nk, T2, KC), f32), pltpu.VMEM((nk, T2, KC), f32), pltpu.VMEM((nk, T2, KC), f32),
            pltpu.VMEM((2, nk, T2, KC), BF),
            pltpu.VMEM((J, T, NC), BF), pltpu.VMEM((J, T, NC), BF), pltpu.VMEM((n, CR, H), f32),
            pltpu.VMEM((J, n, CR, NC), BF), pltpu.VMEM((J, n - 1, CR, NC), BF),
            pltpu.VMEM((J, n, CR, NC), BF), pltpu.VMEM((J, n, CR, NC), BF),
            pltpu.VMEM((2, J, R, NC), BF), pltpu.VMEM((2, 2, J, R, NC), BF),
            pltpu.VMEM((nk, T2, KC), f32), pltpu.VMEM((nk, T2, KC), f32), pltpu.VMEM((nk, T2, KC), f32),
            pltpu.VMEM((2, nk, T2, KC), BF),
            dma, dma((2,)), dma((n, 2)), dma((n, 2)), dma, dma, dma((nk,)), dma((nk,)),
            dma((nk,)), dma((nk,)), dma((J,)), dma((J,)), dma((J, n)), dma((J, n)),
            dma((J, n)), dma((J, n)), dma((J, n)), dma((J, n)), dma((4,)), dma((4,)),
            dma((nk,)), dma((nk,)), dma((nk,)), dma((nk,)), dma((2,)), dma((J,)),
        ],
        compiler_params=pltpu.CompilerParams(
            collective_id=0, has_side_effects=True, vmem_limit_bytes=VMEM_LIMIT),
    )(resid_buf, shuffle.reshape(1, T), mlp_out, enc_weight[0], dec_weight[0], enc_bias, dec_bias)
    fc = 512 if F % 512 == 0 else KC
    enc_grad, dec_grad, bgrad, rebuilt = pl.pallas_call(
        functools.partial(weight_kernel, float(T) ** (-0.5)),
        grid=(F // fc,),
        out_shape=(
            shape((F, H), BF), shape((F, 2, H), BF), shape((1, F), f32), shape((R, 2, 2 * H), BF)),
        in_specs=[
            pl.BlockSpec((T, fc), lambda i: (0, i)), pl.BlockSpec((T, fc), lambda i: (0, i)),
            pl.BlockSpec((2, T, H), lambda i: (0, 0, 0)), pl.BlockSpec((T, H), lambda i: (0, 0)),
            pl.BlockSpec((2 * R, 2 * H), lambda i: (0, 0))],
        out_specs=(
            pl.BlockSpec((fc, H), lambda i: (i, 0)), pl.BlockSpec((fc, 2, H), lambda i: (i, 0, 0)),
            pl.BlockSpec((1, fc), lambda i: (0, i)), pl.BlockSpec((R, 2, 2 * H), lambda i: (0, 0, 0))),
        compiler_params=pltpu.CompilerParams(vmem_limit_bytes=VMEM_LIMIT),
    )(feats, gpre, errs, xs, parts)
    return rebuilt, enc_grad[None], dec_grad[None], bgrad


def chosen(resid_buf, shuffle, mlp_out, enc_weight, dec_weight, enc_bias, dec_bias):
    args = (resid_buf, shuffle, mlp_out, enc_weight, dec_weight, enc_bias, dec_bias)
    rows, width = resid_buf.shape[0], enc_weight.shape[2]
    fits = (
        lax.axis_size("layer") == LAYERS == 2 and lax.axis_size("row") == 2
        and 1 < lax.axis_size("feat") <= 4 and rows % 16 == 0
        and width % KC == 0 and enc_weight.shape[1] % KC == 0)
    return fused(*args) if fits else on_device(*args)


def solution(mesh):
    return jax.shard_map(
        chosen,
        mesh=mesh,
        in_specs=(
            P(("groups", "feat", "row"), None, None),
            P("groups"),
            P(("groups", "feat", "row"), None, None),
            P("layer", "feat", "row"),
            P("layer", "feat", None, "row"),
            P("layer", "feat"),
            P(),
        ),
        out_specs=(
            P(("groups", "feat", "row"), None, None),
            P(("groups", "layer"), "feat", "row"),
            P(("groups", "layer"), "feat", None, "row"),
            P(("groups", "layer"), "feat"),
        ),
        check_vma=False,
    )
```
